32 devices in a mesh: seq: 8 (over z, x), head: 4 (over y, core).
Axes of the slice: x: 2, y: 2, z: 4, core: 2. Of those that a mesh axis runs over, the one named last changes fastest.
Arguments:
- queries: bfloat16 [2048, 2048], P(('seq', 'head')), may hold values from -64 to 64
- keys: bfloat16 [2048, 1024], P(('seq', 'head')), may hold values from -6 to 6
- values: bfloat16 [2048, 1024], P(('seq', 'head')), may hold values from -6 to 6
- output_gradient: bfloat16 [2048, 2048], P(('seq', 'head')), may hold values from -6 to 6
- block_lo: int32 [16], P('seq'), may hold values from 0 to 15, as said below
Outputs:
- attended: bfloat16 [2048, 2048], P(('seq', 'head'))
- query_grads: bfloat16 [2048, 2048], P(('seq', 'head'))
- key_gradient_rows: bfloat16 [2048, 1024], P(('seq', 'head'))
- value_gradient_rows: bfloat16 [2048, 1024], P(('seq', 'head'))
The draws below stay inside these ranges and needn't reach their ends.
Inputs may be any that keep to these rules, and one draw needn't show every extreme that they name: block_lo[b] is the larger of b - 8 and the first block of the document that holds block b; documents begin at block boundaries, block 0 begins one and blocks 1 to 8 begin none; block_lo never falls from one block to the next.
All inputs are finite; a program needn't handle non-finite values.
Results may differ from the reference program's by a relative error of at most 0.025.
Values may be sent and summed in bfloat16 or wider, within the bound.
No kernel may reach another device: no remote copies, remote signals or barrier semaphores. Data moves between devices by JAX's collectives and lax.ppermute only.
A program may use at most 64 MiB of HBM per device.

```python
import jax
import jax.numpy as jnp
from jax import lax

QUERY_HEADS = 16
KEY_VALUE_HEADS = 8
HEAD_SIZE = 128
BLOCK = 128
WBLOCKS = 8
SEQUENCE_TOKENS = 2048
QBLOCKS = 16
WINDOW_TOKENS = 1024


def pair_fields(key):
    base = jax.random.fold_in(key, 7)
    key_query, key_lookup_name = jax.random.split(base, 2)
    queries = jnp.clip(jax.random.normal(key_query, (SEQUENCE_TOKENS, QUERY_HEADS * HEAD_SIZE), jnp.float32), -6.0, 6.0)
    keys = jnp.clip(jax.random.normal(key_lookup_name, (SEQUENCE_TOKENS, KEY_VALUE_HEADS * HEAD_SIZE), jnp.float32), -6.0, 6.0)
    return (queries, keys)


def draw_queries(key, part):
    queries, keys = pair_fields(key)
    return queries.astype(jnp.bfloat16)


def draw_keys(key, part):
    queries, keys = pair_fields(key)
    return keys.astype(jnp.bfloat16)


def draw_block_lo(key, part):
    flag_key = jax.random.fold_in(jax.random.fold_in(key, 11), 1)
    flags = jax.random.randint(flag_key, (QBLOCKS,), 0, 3)
    indices = jnp.arange(QBLOCKS, dtype=jnp.int32)
    starts = (flags == 0) & (indices > WBLOCKS) | (indices == 0)
    first_block = lax.cummax(jnp.where(starts, indices, 0), axis=0)
    return jnp.maximum(indices - WBLOCKS, first_block).astype(jnp.int32)


def steps_of(stream_key, dims, shards, least, top_value):
    def one(position, parts):
        heights = jax.random.uniform(jax.random.fold_in(jax.random.fold_in(stream_key, 6), position), (parts,), jnp.float32, least / len(shards), top_value / len(shards))
        return jnp.repeat(jnp.exp(heights), dims[position] // parts).reshape((-1,) + (1,) * (len(dims) - position - 1))

    level = one(*shards[0])
    for cut in shards[1:]:
        level = level * one(*cut)
    return level


def centred(own_key, extent, spread, bound, shards=(), kind=jnp.bfloat16):
    factor_of = steps_of(own_key, extent, shards, -0.22, 0.18) if shards else 1.0
    values = jax.random.normal(own_key, extent, jnp.float32) * spread * factor_of
    return jnp.minimum(jnp.maximum(values, -bound), bound).astype(kind)


def setup_inputs(seed: int = 0) -> dict:
    streams_of = jax.random.split(jax.random.key(seed), 6)
    queries = draw_queries(jax.random.fold_in(streams_of[5], 71), 0)
    keys = draw_keys(jax.random.fold_in(streams_of[5], 71), 0)
    values = centred(streams_of[2], (SEQUENCE_TOKENS, KEY_VALUE_HEADS * HEAD_SIZE), 1.0, 6.0, ((0, 32),))
    output_gradient = centred(streams_of[3], (SEQUENCE_TOKENS, QUERY_HEADS * HEAD_SIZE), 1.0, 6.0, ((0, 32),))
    block_lo = draw_block_lo(jax.random.fold_in(streams_of[5], 71), 0)
    return dict(queries=queries, keys=keys, values=values, output_gradient=output_gradient, block_lo=block_lo)


query_scale = 168.0 ** -0.5
neg_fill = -1.0e30


def visible_of(q_pos, k_pos, lowest):
    later = k_pos[None, :] <= q_pos[:, None]
    inside = (q_pos[:, None] - k_pos[None, :]) < WINDOW_TOKENS
    above = k_pos[None, :] >= lowest[:, None]
    real_rows = q_pos[:, None] < SEQUENCE_TOKENS
    return later & inside & above & real_rows


def scores_of(query_tile_block, key_tile_block, q_pos, k_pos, lowest):
    queries_per_group = QUERY_HEADS // KEY_VALUE_HEADS
    query_four_axes = query_tile_block.astype(jnp.float32).reshape(query_tile_block.shape[0], KEY_VALUE_HEADS, queries_per_group, HEAD_SIZE)
    key_three_axes = key_tile_block.astype(jnp.float32).reshape(key_tile_block.shape[0], KEY_VALUE_HEADS, HEAD_SIZE)
    scores = jnp.einsum("tngd,knd->ngtk", query_four_axes, key_three_axes) * query_scale
    visible = visible_of(q_pos, k_pos, lowest)
    return jnp.where(visible[None, None], scores, neg_fill)


def to_bf16_f32(array):
    rounded = lax.optimization_barrier(array.astype(jnp.bfloat16))
    return rounded.astype(jnp.float32)


def reference(queries, keys, values, output_gradient, block_lo):
    queries_per_group = QUERY_HEADS // KEY_VALUE_HEADS
    query_extent = 4 * BLOCK
    n_blocks = SEQUENCE_TOKENS // query_extent
    pad_keys = jnp.pad(keys, ((WINDOW_TOKENS, 0), (0, 0)))
    pad_values = jnp.pad(values, ((WINDOW_TOKENS, 0), (0, 0)))
    lowest_rows = jnp.repeat(block_lo.astype(jnp.int32) * BLOCK, BLOCK)

    def forward_block(block_index):
        first_row = (block_index * query_extent).astype(jnp.int32)
        query_tile_block = lax.dynamic_slice_in_dim(queries, first_row, query_extent, 0)
        key_tile_block = lax.dynamic_slice_in_dim(pad_keys, first_row, WINDOW_TOKENS + query_extent, 0)
        value_tile_block = lax.dynamic_slice_in_dim(pad_values, first_row, WINDOW_TOKENS + query_extent, 0)
        q_pos = first_row + jnp.arange(query_extent, dtype=jnp.int32)
        k_pos = first_row - WINDOW_TOKENS + jnp.arange(WINDOW_TOKENS + query_extent, dtype=jnp.int32)
        lowest = lax.dynamic_slice_in_dim(lowest_rows, first_row, query_extent, 0)
        scores = scores_of(query_tile_block, key_tile_block, q_pos, k_pos, lowest)
        row_max = jnp.max(scores, axis=-1, keepdims=True)
        norm_logarithm = row_max + jnp.log(jnp.sum(jnp.exp(scores - row_max), axis=-1, keepdims=True))
        probs = jnp.exp(scores - norm_logarithm)
        value_three_axes = value_tile_block.astype(jnp.float32).reshape(WINDOW_TOKENS + query_extent, KEY_VALUE_HEADS, HEAD_SIZE)
        attended = jnp.einsum("ngtk,knd->tngd", to_bf16_f32(probs), value_three_axes)
        attended = attended.astype(jnp.bfloat16).reshape(query_extent, QUERY_HEADS * HEAD_SIZE)
        return attended, norm_logarithm[..., 0]

    attended, norm_logarithm = lax.map(forward_block, jnp.arange(n_blocks, dtype=jnp.int32))
    attended = attended.reshape(SEQUENCE_TOKENS, QUERY_HEADS * HEAD_SIZE)
    norm_logarithm = jnp.moveaxis(norm_logarithm, 0, 2).reshape(KEY_VALUE_HEADS, queries_per_group, SEQUENCE_TOKENS)
    row_dot_products = jnp.sum(output_gradient.astype(jnp.float32).reshape(SEQUENCE_TOKENS, KEY_VALUE_HEADS, queries_per_group, HEAD_SIZE)
                       * attended.astype(jnp.float32).reshape(SEQUENCE_TOKENS, KEY_VALUE_HEADS, queries_per_group, HEAD_SIZE), axis=-1)
    row_dot_products = jnp.transpose(row_dot_products, (1, 2, 0))

    def query_block(block_index):
        first_row = (block_index * query_extent).astype(jnp.int32)
        query_tile_block = lax.dynamic_slice_in_dim(queries, first_row, query_extent, 0)
        gradient_block = lax.dynamic_slice_in_dim(output_gradient, first_row, query_extent, 0)
        key_tile_block = lax.dynamic_slice_in_dim(pad_keys, first_row, WINDOW_TOKENS + query_extent, 0)
        value_tile_block = lax.dynamic_slice_in_dim(pad_values, first_row, WINDOW_TOKENS + query_extent, 0)
        q_pos = first_row + jnp.arange(query_extent, dtype=jnp.int32)
        k_pos = first_row - WINDOW_TOKENS + jnp.arange(WINDOW_TOKENS + query_extent, dtype=jnp.int32)
        lowest = lax.dynamic_slice_in_dim(lowest_rows, first_row, query_extent, 0)
        scores = scores_of(query_tile_block, key_tile_block, q_pos, k_pos, lowest)
        norm_block = lax.dynamic_slice_in_dim(norm_logarithm, first_row, query_extent, 2)
        dots_block = lax.dynamic_slice_in_dim(row_dot_products, first_row, query_extent, 2)
        probs = jnp.exp(scores - norm_block[..., None])
        gradient_four_axes = gradient_block.astype(jnp.float32).reshape(query_extent, KEY_VALUE_HEADS, queries_per_group, HEAD_SIZE)
        value_three_axes = value_tile_block.astype(jnp.float32).reshape(WINDOW_TOKENS + query_extent, KEY_VALUE_HEADS, HEAD_SIZE)
        key_three_axes = key_tile_block.astype(jnp.float32).reshape(WINDOW_TOKENS + query_extent, KEY_VALUE_HEADS, HEAD_SIZE)
        prob_grads = jnp.einsum("tngd,knd->ngtk", gradient_four_axes, value_three_axes)
        score_grads = to_bf16_f32(probs * (prob_grads - dots_block[..., None]))
        q_grad = query_scale * jnp.einsum("ngtk,knd->tngd", score_grads, key_three_axes)
        return q_grad.astype(jnp.bfloat16).reshape(query_extent, QUERY_HEADS * HEAD_SIZE)

    query_grads = lax.map(query_block, jnp.arange(n_blocks, dtype=jnp.int32)).reshape(SEQUENCE_TOKENS, QUERY_HEADS * HEAD_SIZE)

    pad_queries = jnp.pad(queries, ((0, WINDOW_TOKENS), (0, 0)))
    pad_grads = jnp.pad(output_gradient, ((0, WINDOW_TOKENS), (0, 0)))
    pad_norm = jnp.pad(norm_logarithm, ((0, 0), (0, 0), (0, WINDOW_TOKENS)))
    pad_dots = jnp.pad(row_dot_products, ((0, 0), (0, 0), (0, WINDOW_TOKENS)))
    pad_lowest = jnp.pad(lowest_rows, (0, WINDOW_TOKENS))

    def key_block(block_index):
        first_row = (block_index * query_extent).astype(jnp.int32)
        key_tile_block = lax.dynamic_slice_in_dim(keys, first_row, query_extent, 0)
        value_tile_block = lax.dynamic_slice_in_dim(values, first_row, query_extent, 0)
        query_tile_block = lax.dynamic_slice_in_dim(pad_queries, first_row, query_extent + WINDOW_TOKENS, 0)
        gradient_block = lax.dynamic_slice_in_dim(pad_grads, first_row, query_extent + WINDOW_TOKENS, 0)
        q_pos = first_row + jnp.arange(query_extent + WINDOW_TOKENS, dtype=jnp.int32)
        k_pos = first_row + jnp.arange(query_extent, dtype=jnp.int32)
        lowest = lax.dynamic_slice_in_dim(pad_lowest, first_row, query_extent + WINDOW_TOKENS, 0)
        scores = scores_of(query_tile_block, key_tile_block, q_pos, k_pos, lowest)
        norm_block = lax.dynamic_slice_in_dim(pad_norm, first_row, query_extent + WINDOW_TOKENS, 2)
        dots_block = lax.dynamic_slice_in_dim(pad_dots, first_row, query_extent + WINDOW_TOKENS, 2)
        probs = jnp.exp(scores - norm_block[..., None])
        gradient_four_axes = gradient_block.astype(jnp.float32).reshape(query_extent + WINDOW_TOKENS, KEY_VALUE_HEADS, queries_per_group, HEAD_SIZE)
        query_four_axes = query_tile_block.astype(jnp.float32).reshape(query_extent + WINDOW_TOKENS, KEY_VALUE_HEADS, queries_per_group, HEAD_SIZE)
        value_three_axes = value_tile_block.astype(jnp.float32).reshape(query_extent, KEY_VALUE_HEADS, HEAD_SIZE)
        prob_grads = jnp.einsum("tngd,knd->ngtk", gradient_four_axes, value_three_axes)
        score_grads = to_bf16_f32(probs * (prob_grads - dots_block[..., None]))
        value_gradient = jnp.einsum("ngtk,tngd->knd", to_bf16_f32(probs), gradient_four_axes)
        key_gradient = query_scale * jnp.einsum("ngtk,tngd->knd", score_grads, query_four_axes)
        return (key_gradient.astype(jnp.bfloat16).reshape(query_extent, KEY_VALUE_HEADS * HEAD_SIZE),
                value_gradient.astype(jnp.bfloat16).reshape(query_extent, KEY_VALUE_HEADS * HEAD_SIZE))

    key_gradient_rows, value_gradient_rows = lax.map(key_block, jnp.arange(n_blocks, dtype=jnp.int32))
    key_gradient_rows = key_gradient_rows.reshape(SEQUENCE_TOKENS, KEY_VALUE_HEADS * HEAD_SIZE)
    value_gradient_rows = value_gradient_rows.reshape(SEQUENCE_TOKENS, KEY_VALUE_HEADS * HEAD_SIZE)
    return attended, query_grads, key_gradient_rows, value_gradient_rows
```

```python
import functools

import jax
import jax.numpy as jnp
from jax import lax
from jax.experimental import pallas as pl
from jax.experimental.pallas import tpu as pltpu
from jax.sharding import Mesh, PartitionSpec as P

HEAD_SIZE = 128
BLOCK = 128
WBLOCKS = 8
LOG2E = 1.4426950408889634

query_scale = 168.0 ** (-0.5)
neg_fill = -1e30
EXTRA = 8

VM = pl.BlockSpec(memory_space=pltpu.VMEM)
SM = pl.BlockSpec(memory_space=pltpu.SMEM)


def pack_kv_kernel(k_ref, v_ref, o_ref):
    n = o_ref.shape[0]
    for i in range(n):
        cols = slice(i * HEAD_SIZE, (i + 1) * HEAD_SIZE)
        o_ref[i, :, :HEAD_SIZE] = k_ref[:, cols]
        o_ref[i, :, HEAD_SIZE:] = v_ref[:, cols]


def pack_qg_kernel(base_ref, lo_ref, q_ref, g_ref, o_ref):
    n, rows, _ = o_ref.shape
    rows -= EXTRA
    wide = q_ref.shape[1] // n
    for i in range(n):
        cols = slice(i * wide, (i + 1) * wide)
        o_ref[i, :rows, :wide] = q_ref[:, cols]
        o_ref[i, :rows, wide:] = g_ref[:, cols]
    lane = lax.broadcasted_iota(jnp.int32, (EXTRA, 2 * wide), 1)
    told = jnp.zeros((EXTRA, 2 * wide), jnp.float32)
    for j in range(lo_ref.shape[0]):
        back = (base_ref[0] + j - lo_ref[j]).astype(jnp.float32)
        told = jnp.where(lane // BLOCK == j, back, told)
    for i in range(n):
        o_ref[i, rows:, :] = told.astype(jnp.bfloat16)


def attention_kernel(head_count, qg_ref, kv0_ref, kv1_ref, kv2_ref,
                     od_ref, g0_ref, g1_ref, g2_ref, k_s, v_s, dk_s, dv_s):
    n, rows, _ = kv0_ref.shape
    tok = n * rows
    blocks = tok // BLOCK
    for part, ref in enumerate((kv2_ref, kv1_ref, kv0_ref)):
        k_s[part * tok : (part + 1) * tok] = ref[:, :, :HEAD_SIZE].reshape(tok, HEAD_SIZE)
        v_s[part * tok : (part + 1) * tok] = ref[:, :, HEAD_SIZE:].reshape(tok, HEAD_SIZE)
    dk_s[...] = jnp.zeros_like(dk_s)
    dv_s[...] = jnp.zeros_like(dv_s)
    span = (WBLOCKS + 1) * BLOCK
    per = BLOCK // rows
    seq_blocks = head_count * rows // BLOCK
    col = lax.broadcasted_iota(jnp.int32, (BLOCK, span), 1)
    row = lax.broadcasted_iota(jnp.int32, (BLOCK, span), 0)
    band = (col > row) & (col <= row + WBLOCKS * BLOCK)
    hi = lax.axis_index("hi")
    for i in range(blocks):
        first = 2 * tok + (i - WBLOCKS) * BLOCK
        keys = slice(first, first + span)
        chunk = slice(i * per, (i + 1) * per)

        def head_of(j):
            return qg_ref[chunk, :rows, j * HEAD_SIZE : (j + 1) * HEAD_SIZE].reshape(
                BLOCK, HEAD_SIZE
            )

        q = jnp.concatenate([head_of(0), head_of(1)], axis=0)
        g = jnp.concatenate([head_of(2), head_of(3)], axis=0)
        owner = (i // seq_blocks) * head_count
        lane = (i % seq_blocks) * BLOCK
        back = qg_ref[owner, rows : rows + 1, lane : lane + 1].astype(jnp.float32)
        least = jnp.maximum(
            (WBLOCKS - back) * BLOCK,
            (WBLOCKS - (hi * blocks + i)).astype(jnp.float32) * BLOCK,
        )
        seen = band & (col.astype(jnp.float32) >= least)
        seen = jnp.concatenate([seen, seen], axis=0)
        k = k_s[keys]
        v = v_s[keys]
        s = lax.dot_general(q, k, (((1,), (1,)), ((), ())), preferred_element_type=jnp.float32)
        s = jnp.where(seen, s * (query_scale * LOG2E), neg_fill)
        e = jnp.exp2(s - jnp.max(s, axis=1, keepdims=True))
        p = e * (1.0 / jnp.sum(e, axis=1, keepdims=True))
        pb = p.astype(jnp.bfloat16)
        o = jnp.dot(pb, v, preferred_element_type=jnp.float32).astype(jnp.bfloat16)
        dots = jnp.sum(g.astype(jnp.float32) * o.astype(jnp.float32), axis=1, keepdims=True)
        dp = lax.dot_general(g, v, (((1,), (1,)), ((), ())), preferred_element_type=jnp.float32)
        ds = (p * (dp - dots)).astype(jnp.bfloat16)
        dq = (query_scale * jnp.dot(ds, k, preferred_element_type=jnp.float32)).astype(jnp.bfloat16)
        dk_s[keys] += lax.dot_general(
            ds, q, (((0,), (0,)), ((), ())), preferred_element_type=jnp.float32
        )
        dv_s[keys] += lax.dot_general(
            pb, g, (((0,), (0,)), ((), ())), preferred_element_type=jnp.float32
        )
        for u in range(2):
            part = slice(u * BLOCK, (u + 1) * BLOCK)
            od_ref[chunk, :, u * HEAD_SIZE : (u + 1) * HEAD_SIZE] = o[part].reshape(
                per, rows, HEAD_SIZE
            )
            od_ref[chunk, :, (2 + u) * HEAD_SIZE : (3 + u) * HEAD_SIZE] = dq[part].reshape(
                per, rows, HEAD_SIZE
            )
    for part, ref in enumerate((g2_ref, g1_ref, g0_ref)):
        own = slice(part * tok, (part + 1) * tok)
        ref[:, :, :HEAD_SIZE] = (
            (query_scale * dk_s[own]).astype(ref.dtype).reshape(n, rows, HEAD_SIZE)
        )
        ref[:, :, HEAD_SIZE:] = dv_s[own].astype(ref.dtype).reshape(n, rows, HEAD_SIZE)


def add_kernel(a_ref, b_ref, o_ref):
    o_ref[...] = (a_ref[...].astype(jnp.float32) + b_ref[...].astype(jnp.float32)).astype(
        jnp.bfloat16
    )


def unpack_kernel(a_ref, x_ref, y_ref):
    n = a_ref.shape[0]
    wide = a_ref.shape[2] // 2
    for i in range(n):
        x_ref[:, i * wide : (i + 1) * wide] = a_ref[i, :, :wide]
        y_ref[:, i * wide : (i + 1) * wide] = a_ref[i, :, wide:]


def call(kernel, outs, args, scratch=(), smem=0):
    return pl.pallas_call(
        kernel,
        out_shape=outs,
        in_specs=[SM] * smem + [VM] * (len(args) - smem),
        out_specs=jax.tree.map(lambda _: VM, outs),
        scratch_shapes=list(scratch),
    )(*args)


def ring(x, by):
    n = lax.axis_size("hi")
    return lax.ppermute(x, "hi", [(i, (i + by) % n) for i in range(n)])


def exchange(x):
    return lax.all_to_all(x, ("lo", "head"), split_axis=0, concat_axis=0, tiled=True)


def body(queries, keys, values, output_gradient, block_lo):
    rows = queries.shape[0]
    n = lax.axis_size("lo") * lax.axis_size("head")
    tok = n * rows
    heads = lax.axis_size("head")
    bf = functools.partial(jax.ShapeDtypeStruct, dtype=jnp.bfloat16)
    f32 = functools.partial(jax.ShapeDtypeStruct, dtype=jnp.float32)
    seq = lax.axis_index("hi") * lax.axis_size("lo") + lax.axis_index("lo")
    base = (seq * block_lo.shape[0]).astype(jnp.int32).reshape(1)

    kv_out = call(pack_kv_kernel, bf((n, rows, 2 * HEAD_SIZE)), (keys, values))
    qg_out = call(
        pack_qg_kernel,
        bf((n, rows + EXTRA, 4 * HEAD_SIZE)),
        (base, block_lo, queries, output_gradient),
        smem=2,
    )
    kv0 = exchange(kv_out)
    kv1 = ring(kv0, 1)
    kv0, qg_out = lax.optimization_barrier((kv0, qg_out))
    qg = exchange(qg_out)
    kv2 = ring(kv1, 1)
    od, g0, g1, g2 = call(
        functools.partial(attention_kernel, heads),
        (
            bf((n, rows, 4 * HEAD_SIZE)),
            f32((n, rows, 2 * HEAD_SIZE)),
            f32((n, rows, 2 * HEAD_SIZE)),
            bf((n, rows, 2 * HEAD_SIZE)),
        ),
        (qg, kv0, kv1, kv2),
        scratch=[
            pltpu.VMEM((3 * tok, HEAD_SIZE), jnp.bfloat16),
            pltpu.VMEM((3 * tok, HEAD_SIZE), jnp.bfloat16),
            pltpu.VMEM((3 * tok, HEAD_SIZE), jnp.float32),
            pltpu.VMEM((3 * tok, HEAD_SIZE), jnp.float32),
        ],
    )
    r1 = ring(g2, -1)
    od_in = exchange(od)
    t = call(add_kernel, bf(g1.shape), (g1, r1))
    r2 = ring(t, -1)
    final = call(add_kernel, bf(g0.shape), (g0, r2))
    g_in = exchange(final)
    attended, query_grads = call(
        unpack_kernel, (bf((rows, 2 * tok // rows * HEAD_SIZE)),) * 2, (od_in,)
    )
    key_grads, value_grads = call(
        unpack_kernel, (bf((rows, tok // rows * HEAD_SIZE)),) * 2, (g_in,)
    )
    return attended, query_grads, key_grads, value_grads


def solution(mesh):
    seq, head = mesh.devices.shape
    kv_heads = 8
    lo = kv_heads // head
    inner = Mesh(mesh.devices.reshape(seq // lo, lo, head), ("hi", "lo", "head"))
    tokens = P(("hi", "lo", "head"), None)
    return jax.shard_map(
        body,
        mesh=inner,
        in_specs=(tokens,) * 4 + (P(("hi", "lo")),),
        out_specs=(tokens,) * 4,
        check_vma=False,
    )
```

```python
import functools

import jax
import jax.numpy as jnp
from jax import lax
from jax.experimental import pallas as pl
from jax.experimental.pallas import tpu as pltpu
from jax.sharding import Mesh, PartitionSpec as P

HEAD_SIZE = 128
BLOCK = 128
WBLOCKS = 8
LOG2E = 1.4426950408889634

query_scale = 168.0 ** (-0.5)
neg_fill = -1e30
EXTRA = 8

VM = pl.BlockSpec(memory_space=pltpu.VMEM)
SM = pl.BlockSpec(memory_space=pltpu.SMEM)
HB = pl.BlockSpec(memory_space=pl.ANY)


def copy_all(pairs, sems):
    copies = [
        pltpu.make_async_copy(src, dst, sems.at[i]) for i, (src, dst) in enumerate(pairs)
    ]
    for copy in copies:
        copy.start()
    return copies


def pack_kv_kernel(k_ref, v_ref, o_ref, sems):
    pairs = []
    for i in range(o_ref.shape[0]):
        cols = slice(i * HEAD_SIZE, (i + 1) * HEAD_SIZE)
        pairs.append((k_ref.at[:, cols], o_ref.at[i, :, :HEAD_SIZE]))
        pairs.append((v_ref.at[:, cols], o_ref.at[i, :, HEAD_SIZE:]))
    for copy in copy_all(pairs, sems):
        copy.wait()


def pack_qg_kernel(base_ref, lo_ref, q_ref, g_ref, o_ref, sems):
    n, rows, _ = o_ref.shape
    rows -= EXTRA
    wide = q_ref.shape[1] // n
    pairs = []
    for i in range(n):
        cols = slice(i * wide, (i + 1) * wide)
        pairs.append((q_ref.at[:, cols], o_ref.at[i, :rows, :wide]))
        pairs.append((g_ref.at[:, cols], o_ref.at[i, :rows, wide:]))
    copies = copy_all(pairs, sems)
    lane = lax.broadcasted_iota(jnp.int32, (EXTRA, 2 * wide), 1)
    told = jnp.zeros((EXTRA, 2 * wide), jnp.float32)
    for j in range(lo_ref.shape[0]):
        back = (base_ref[0] + j - lo_ref[j]).astype(jnp.float32)
        told = jnp.where(lane // BLOCK == j, back, told)
    for i in range(n):
        o_ref[i, rows:, :] = told.astype(jnp.bfloat16)
    for copy in copies:
        copy.wait()


def stacked(qg_ref, i, rows, first):
    per = BLOCK // rows
    return jnp.concatenate(
        [
            qg_ref[i * per : (i + 1) * per, :rows, j * HEAD_SIZE : (j + 1) * HEAD_SIZE].reshape(
                BLOCK, HEAD_SIZE
            )
            for j in (first, first + 1)
        ],
        axis=0,
    )


def nt(a, b):
    return lax.dot_general(a, b, (((1,), (1,)), ((), ())), preferred_element_type=jnp.float32)


def tn(a, b):
    return lax.dot_general(a, b, (((0,), (0,)), ((), ())), preferred_element_type=jnp.float32)


def nn(a, b):
    return jnp.dot(a, b, preferred_element_type=jnp.float32)


def forward_kernel(head_count, qg_ref, kv0_ref, kv1_ref, kv2_ref,
                   k_s, v_s, o_ref, p_ref, dsf_ref, dots_ref, g2_ref, dk_s, dv_s):
    n, rows, _ = kv0_ref.shape
    tok = n * rows
    blocks = tok // BLOCK
    for part, ref in enumerate((kv2_ref, kv1_ref, kv0_ref)):
        k_s[part * tok : (part + 1) * tok] = ref[:, :, :HEAD_SIZE].reshape(tok, HEAD_SIZE)
        v_s[part * tok : (part + 1) * tok] = ref[:, :, HEAD_SIZE:].reshape(tok, HEAD_SIZE)
    dk_s[...] = jnp.zeros_like(dk_s)
    dv_s[...] = jnp.zeros_like(dv_s)
    span = (WBLOCKS + 1) * BLOCK
    seq_blocks = head_count * rows // BLOCK
    col = lax.broadcasted_iota(jnp.int32, (BLOCK, span), 1)
    row = lax.broadcasted_iota(jnp.int32, (BLOCK, span), 0)
    band = (col > row) & (col <= row + WBLOCKS * BLOCK)
    hi = lax.axis_index("hi")
    for i in range(blocks):
        first = 2 * tok + (i - WBLOCKS) * BLOCK
        keys = slice(first, first + span)
        far = slice(first, tok)
        width = tok - first
        q = stacked(qg_ref, i, rows, 0)
        g = stacked(qg_ref, i, rows, 2)
        owner = (i // seq_blocks) * head_count
        lane = (i % seq_blocks) * BLOCK
        back = qg_ref[owner, rows : rows + 1, lane : lane + 1].astype(jnp.float32)
        least = jnp.maximum(
            (WBLOCKS - back) * BLOCK,
            (WBLOCKS - (hi * blocks + i)).astype(jnp.float32) * BLOCK,
        )
        seen = band & (col.astype(jnp.float32) >= least)
        seen = jnp.concatenate([seen, seen], axis=0)
        s = jnp.where(seen, nt(q, k_s[keys]) * (query_scale * LOG2E), neg_fill)
        e = jnp.exp2(s - jnp.max(s, axis=1, keepdims=True))
        p = e * (1.0 / jnp.sum(e, axis=1, keepdims=True))
        pb = p.astype(jnp.bfloat16)
        o = nn(pb, v_s[keys]).astype(jnp.bfloat16)
        dots = jnp.sum(g.astype(jnp.float32) * o.astype(jnp.float32), axis=1, keepdims=True)
        o_ref[i] = o
        p_ref[i, :, width:] = pb[:, width:]
        dots_ref[i] = jnp.broadcast_to(dots, (2 * BLOCK, HEAD_SIZE))
        ds = (p[:, :width] * (nt(g, v_s[far]) - dots)).astype(jnp.bfloat16)
        dsf_ref[i, :, :width] = ds
        dk_s[far] += tn(ds, q)
        dv_s[far] += tn(pb[:, :width], g)
    g2_ref[:, :, :HEAD_SIZE] = (
        (query_scale * dk_s[...]).astype(jnp.bfloat16).reshape(n, rows, HEAD_SIZE)
    )
    g2_ref[:, :, HEAD_SIZE:] = dv_s[...].astype(jnp.bfloat16).reshape(n, rows, HEAD_SIZE)


def backward_kernel(qg_ref, k_s, v_s, o_ref, p_ref, dsf_ref, dots_ref,
                    od_ref, g1_ref, g0_ref, dk_s, dv_s):
    n, rows, _ = od_ref.shape
    tok = n * rows
    blocks = tok // BLOCK
    per = BLOCK // rows
    dk_s[...] = jnp.zeros_like(dk_s)
    dv_s[...] = jnp.zeros_like(dv_s)
    for i in range(blocks):
        first = 2 * tok + (i - WBLOCKS) * BLOCK
        last = first + (WBLOCKS + 1) * BLOCK
        width = tok - first
        near = slice(tok, last)
        here = slice(0, last - tok)
        q = stacked(qg_ref, i, rows, 0)
        g = stacked(qg_ref, i, rows, 2)
        pb = p_ref[i, :, width:]
        dots = dots_ref[i, :, :1]
        ds = (pb.astype(jnp.float32) * (nt(g, v_s[near]) - dots)).astype(jnp.bfloat16)
        dq = nn(ds, k_s[near]) + nn(dsf_ref[i, :, :width], k_s[first:tok])
        dq = (query_scale * dq).astype(jnp.bfloat16)
        o = o_ref[i]
        dk_s[here] += tn(ds, q)
        dv_s[here] += tn(pb, g)
        chunk = slice(i * per, (i + 1) * per)
        for u in range(2):
            part = slice(u * BLOCK, (u + 1) * BLOCK)
            od_ref[chunk, :, u * HEAD_SIZE : (u + 1) * HEAD_SIZE] = o[part].reshape(
                per, rows, HEAD_SIZE
            )
            od_ref[chunk, :, (2 + u) * HEAD_SIZE : (3 + u) * HEAD_SIZE] = dq[part].reshape(
                per, rows, HEAD_SIZE
            )
    for part, ref in enumerate((g1_ref, g0_ref)):
        own = slice(part * tok, (part + 1) * tok)
        ref[:, :, :HEAD_SIZE] = (query_scale * dk_s[own]).reshape(n, rows, HEAD_SIZE)
        ref[:, :, HEAD_SIZE:] = dv_s[own].reshape(n, rows, HEAD_SIZE)


def add_kernel(a_ref, b_ref, o_ref):
    o_ref[...] = (a_ref[...] + b_ref[...].astype(jnp.float32)).astype(jnp.bfloat16)


def unpack_kernel(a_ref, x_ref, y_ref, sems):
    wide = a_ref.shape[2] // 2
    pairs = []
    for i in range(a_ref.shape[0]):
        cols = slice(i * wide, (i + 1) * wide)
        pairs.append((a_ref.at[i, :, :wide], x_ref.at[:, cols]))
        pairs.append((a_ref.at[i, :, wide:], y_ref.at[:, cols]))
    for copy in copy_all(pairs, sems):
        copy.wait()


def call(kernel, outs, args, scratch=(), smem=0, outer=0, room=2):
    held = [
        x if i < smem + outer else pltpu.with_memory_space_constraint(x, pltpu.VMEM)
        for i, x in enumerate(args)
    ]
    return pl.pallas_call(
        kernel,
        out_shape=outs,
        in_specs=[SM] * smem + [HB] * outer + [VM] * (len(args) - smem - outer),
        out_specs=jax.tree.map(
            lambda o: HB if isinstance(o, jax.ShapeDtypeStruct) else VM,
            outs,
            is_leaf=lambda o: not isinstance(o, tuple),
        ),
        scratch_shapes=list(scratch),
        compiler_params=pltpu.CompilerParams(vmem_limit_bytes=room << 20),
    )(*held)


def ring(x, by):
    n = lax.axis_size("hi")
    return lax.ppermute(x, "hi", [(i, (i + by) % n) for i in range(n)])


def exchange(x):
    return lax.all_to_all(x, ("lo", "head"), split_axis=0, concat_axis=0, tiled=True)


def bf(*shape):
    return pltpu.VMEM(shape, jnp.bfloat16)


def f32(*shape):
    return pltpu.VMEM(shape, jnp.float32)


def out(*shape):
    return jax.ShapeDtypeStruct(shape, jnp.bfloat16)


def body(queries, keys, values, output_gradient, block_lo):
    rows = queries.shape[0]
    n = lax.axis_size("lo") * lax.axis_size("head")
    tok = n * rows
    blocks = tok // BLOCK
    heads = lax.axis_size("head")
    span = (WBLOCKS + 1) * BLOCK
    seq = lax.axis_index("hi") * lax.axis_size("lo") + lax.axis_index("lo")
    base = (seq * block_lo.shape[0]).astype(jnp.int32).reshape(1)
    sems = pltpu.SemaphoreType.DMA((2 * n,))

    kv_out = call(
        pack_kv_kernel, bf(n, rows, 2 * HEAD_SIZE), (keys, values), scratch=[sems], outer=2
    )
    qg_out = call(
        pack_qg_kernel,
        bf(n, rows + EXTRA, 4 * HEAD_SIZE),
        (base, block_lo, queries, output_gradient),
        scratch=[sems],
        smem=2,
        outer=2,
    )
    kv0 = exchange(kv_out)
    kv1 = ring(kv0, 1)
    kv0, qg_out = lax.optimization_barrier((kv0, qg_out))
    qg = exchange(qg_out)
    kv2 = ring(kv1, 1)
    k_all, v_all, o, p, dsf, dots, g2 = call(
        functools.partial(forward_kernel, heads),
        (
            bf(3 * tok, HEAD_SIZE),
            bf(3 * tok, HEAD_SIZE),
            bf(blocks, 2 * BLOCK, HEAD_SIZE),
            bf(blocks, 2 * BLOCK, span),
            bf(blocks, 2 * BLOCK, tok),
            f32(blocks, 2 * BLOCK, HEAD_SIZE),
            bf(n, rows, 2 * HEAD_SIZE),
        ),
        (qg, kv0, kv1, kv2),
        scratch=[f32(tok, HEAD_SIZE), f32(tok, HEAD_SIZE)],
        room=24,
    )
    r1 = ring(g2, -1)
    od, g1, g0 = call(
        backward_kernel,
        (
            bf(n, rows, 4 * HEAD_SIZE),
            f32(n, rows, 2 * HEAD_SIZE),
            f32(n, rows, 2 * HEAD_SIZE),
        ),
        (qg, k_all, v_all, o, p, dsf, dots),
        scratch=[f32(2 * tok, HEAD_SIZE), f32(2 * tok, HEAD_SIZE)],
        room=24,
    )
    od_in = exchange(od)
    t = call(add_kernel, bf(*g1.shape), (g1, r1))
    r2 = ring(t, -1)
    final = call(add_kernel, bf(*g0.shape), (g0, r2))
    g_in = exchange(final)
    attended, query_grads = call(
        unpack_kernel, (out(rows, 2 * n * HEAD_SIZE),) * 2, (od_in,), scratch=[sems]
    )
    key_grads, value_grads = call(
        unpack_kernel, (out(rows, n * HEAD_SIZE),) * 2, (g_in,), scratch=[sems]
    )
    return attended, query_grads, key_grads, value_grads


def solution(mesh):
    seq, head = mesh.devices.shape
    kv_heads = 8
    lo = kv_heads // head
    inner = Mesh(mesh.devices.reshape(seq // lo, lo, head), ("hi", "lo", "head"))
    tokens = P(("hi", "lo", "head"), None)
    return jax.shard_map(
        body,
        mesh=inner,
        in_specs=(tokens,) * 4 + (P(("hi", "lo")),),
        out_specs=(tokens,) * 4,
        check_vma=False,
    )
```

```python
import functools

import jax
import jax.numpy as jnp
from jax import lax
from jax.experimental import pallas as pl
from jax.experimental.pallas import tpu as pltpu
from jax.sharding import Mesh, PartitionSpec as P

HEAD_SIZE = 128
BLOCK = 128
WBLOCKS = 8
LOG2E = 1.4426950408889634

query_scale = 168.0 ** (-0.5)
neg_fill = -1e30
EXTRA = 8

VM = pl.BlockSpec(memory_space=pltpu.VMEM)
HB = pl.BlockSpec(memory_space=pl.ANY)


def copy_all(pairs, sems):
    copies = [
        pltpu.make_async_copy(src, dst, sems.at[i]) for i, (src, dst) in enumerate(pairs)
    ]
    for copy in copies:
        copy.start()
    return copies


def pack_kernel(lo_ref, q_ref, k_ref, v_ref, g_ref, kv_ref, qg_ref, told_s, lo_s, lo_sem, sems):
    n, rows, _ = kv_ref.shape
    wide = q_ref.shape[1] // n
    fetch = pltpu.make_async_copy(lo_ref, lo_s, lo_sem)
    fetch.start()
    pairs = []
    for i in range(n):
        cols = slice(i * HEAD_SIZE, (i + 1) * HEAD_SIZE)
        pairs.append((k_ref.at[:, cols], kv_ref.at[i, :, :HEAD_SIZE]))
        pairs.append((v_ref.at[:, cols], kv_ref.at[i, :, HEAD_SIZE:]))
    for i in range(n):
        cols = slice(i * wide, (i + 1) * wide)
        pairs.append((q_ref.at[:, cols], qg_ref.at[i, :rows, :wide]))
        pairs.append((g_ref.at[:, cols], qg_ref.at[i, :rows, wide:]))
    copies = copy_all(pairs, sems)
    fetch.wait()
    shards = lo_ref.shape[0]
    base = (lax.axis_index("hi") * lax.axis_size("lo") + lax.axis_index("lo")) * shards
    lane = lax.broadcasted_iota(jnp.int32, told_s.shape, 1)
    told = jnp.zeros(told_s.shape, jnp.float32)
    for j in range(shards):
        back = (base + j - lo_s[j]).astype(jnp.float32)
        told = jnp.where(lane // BLOCK == j, back, told)
    told_s[...] = told.astype(jnp.bfloat16)
    more = copy_all(
        [(told_s, qg_ref.at[i, rows:, :]) for i in range(n)], sems.at[pl.ds(4 * n, n)]
    )
    for copy in copies + more:
        copy.wait()


def stacked(qg_ref, i, rows, first):
    per = BLOCK // rows
    return jnp.concatenate(
        [
            qg_ref[i * per : (i + 1) * per, :rows, j * HEAD_SIZE : (j + 1) * HEAD_SIZE].reshape(
                BLOCK, HEAD_SIZE
            )
            for j in (first, first + 1)
        ],
        axis=0,
    )


def nt(a, b):
    return lax.dot_general(a, b, (((1,), (1,)), ((), ())), preferred_element_type=jnp.float32)


def tn(a, b):
    return lax.dot_general(a, b, (((0,), (0,)), ((), ())), preferred_element_type=jnp.float32)


def nn(a, b):
    return jnp.dot(a, b, preferred_element_type=jnp.float32)


def forward_kernel(head_count, qg_ref, kv0_ref, kv1_ref, kv2_ref,
                   k_s, v_s, o_ref, gs_ref, p_ref, dsf_ref, dots_ref, g2_ref, dk_s, dv_s):
    n, rows, _ = kv0_ref.shape
    tok = n * rows
    blocks = tok // BLOCK
    for part, ref in enumerate((kv2_ref, kv1_ref, kv0_ref)):
        k_s[part * tok : (part + 1) * tok] = ref[:, :, :HEAD_SIZE].reshape(tok, HEAD_SIZE)
        v_s[part * tok : (part + 1) * tok] = ref[:, :, HEAD_SIZE:].reshape(tok, HEAD_SIZE)
    dk_s[...] = jnp.zeros_like(dk_s)
    dv_s[...] = jnp.zeros_like(dv_s)
    seq_blocks = head_count * rows // BLOCK
    col = lax.broadcasted_iota(jnp.int32, (2 * BLOCK, BLOCK), 1)
    row = lax.broadcasted_iota(jnp.int32, (2 * BLOCK, BLOCK), 0) % BLOCK
    hi = lax.axis_index("hi")
    scale = query_scale * LOG2E
    for i in range(blocks):
        first = 2 * tok + (i - WBLOCKS) * BLOCK
        keys = slice(first, first + (WBLOCKS + 1) * BLOCK)
        far = slice(first, tok)
        width = tok - first
        q = stacked(qg_ref, i, rows, 0)
        g = stacked(qg_ref, i, rows, 2)
        owner = (i // seq_blocks) * head_count
        lane = (i % seq_blocks) * BLOCK
        back = qg_ref[owner, rows : rows + 1, lane : lane + 1].astype(jnp.float32)
        back = jnp.minimum(back, (hi * blocks + i).astype(jnp.float32))
        s = nt(q, k_s[keys])
        parts = []
        for j in range(WBLOCKS + 1):
            part = s[:, j * BLOCK : (j + 1) * BLOCK]
            if j == WBLOCKS:
                part = jnp.where(col <= row, part, neg_fill)
            else:
                part = part + jnp.where(back < WBLOCKS - j, neg_fill, 0.0)
            if j == 0:
                part = jnp.where(col > row, part, neg_fill)
            parts.append(part)
        top = jnp.max(functools.reduce(jnp.maximum, parts), axis=1, keepdims=True)
        parts = [jnp.exp2((part - top) * scale) for part in parts]
        share = 1.0 / jnp.sum(functools.reduce(jnp.add, parts), axis=1, keepdims=True)
        e = jnp.concatenate(parts, axis=1)
        eb = e.astype(jnp.bfloat16)
        o = (nn(eb, v_s[keys]) * share).astype(jnp.bfloat16)
        dots = jnp.sum(g.astype(jnp.float32) * o.astype(jnp.float32), axis=1, keepdims=True)
        dots = dots * share
        g = (g.astype(jnp.float32) * share).astype(jnp.bfloat16)
        o_ref[i] = o
        gs_ref[i] = g
        p_ref[i, :, width:] = eb[:, width:]
        dots_ref[i] = jnp.broadcast_to(dots, (2 * BLOCK, HEAD_SIZE))
        ds = (e[:, :width] * (nt(g, v_s[far]) - dots)).astype(jnp.bfloat16)
        dsf_ref[i, :, :width] = ds
        dk_s[far] += tn(ds, q)
        dv_s[far] += tn(eb[:, :width], g)
    g2_ref[:, :, :HEAD_SIZE] = (
        (query_scale * dk_s[...]).astype(jnp.bfloat16).reshape(n, rows, HEAD_SIZE)
    )
    g2_ref[:, :, HEAD_SIZE:] = dv_s[...].astype(jnp.bfloat16).reshape(n, rows, HEAD_SIZE)


def backward_kernel(qg_ref, k_s, v_s, o_ref, gs_ref, p_ref, dsf_ref, dots_ref,
                    od_ref, g1_ref, g0_ref, dk_s, dv_s):
    n, rows, _ = od_ref.shape
    tok = n * rows
    blocks = tok // BLOCK
    per = BLOCK // rows
    dk_s[...] = jnp.zeros_like(dk_s)
    dv_s[...] = jnp.zeros_like(dv_s)
    for i in range(blocks):
        first = 2 * tok + (i - WBLOCKS) * BLOCK
        last = first + (WBLOCKS + 1) * BLOCK
        width = tok - first
        near = slice(tok, last)
        here = slice(0, last - tok)
        q = stacked(qg_ref, i, rows, 0)
        g = gs_ref[i]
        pb = p_ref[i, :, width:]
        dots = dots_ref[i, :, :1]
        ds = (pb.astype(jnp.float32) * (nt(g, v_s[near]) - dots)).astype(jnp.bfloat16)
        dq = nn(ds, k_s[near]) + nn(dsf_ref[i, :, :width], k_s[first:tok])
        dq = (query_scale * dq).astype(jnp.bfloat16)
        o = o_ref[i]
        dk_s[here] += tn(ds, q)
        dv_s[here] += tn(pb, g)
        chunk = slice(i * per, (i + 1) * per)
        for u in range(2):
            part = slice(u * BLOCK, (u + 1) * BLOCK)
            od_ref[chunk, :, u * HEAD_SIZE : (u + 1) * HEAD_SIZE] = o[part].reshape(
                per, rows, HEAD_SIZE
            )
            od_ref[chunk, :, (2 + u) * HEAD_SIZE : (3 + u) * HEAD_SIZE] = dq[part].reshape(
                per, rows, HEAD_SIZE
            )
    for part, ref in enumerate((g1_ref, g0_ref)):
        own = slice(part * tok, (part + 1) * tok)
        ref[:, :, :HEAD_SIZE] = (query_scale * dk_s[own]).reshape(n, rows, HEAD_SIZE)
        ref[:, :, HEAD_SIZE:] = dv_s[own].reshape(n, rows, HEAD_SIZE)


def add_kernel(a_ref, b_ref, o_ref):
    o_ref[...] = (a_ref[...] + b_ref[...].astype(jnp.float32)).astype(jnp.bfloat16)


def unpack_kernel(a_ref, b_ref, o_ref, dq_ref, dk_ref, dv_ref, sems):
    pairs = []
    for ref, left, right in ((a_ref, o_ref, dq_ref), (b_ref, dk_ref, dv_ref)):
        wide = ref.shape[2] // 2
        for i in range(ref.shape[0]):
            cols = slice(i * wide, (i + 1) * wide)
            pairs.append((ref.at[i, :, :wide], left.at[:, cols]))
            pairs.append((ref.at[i, :, wide:], right.at[:, cols]))
    for copy in copy_all(pairs, sems):
        copy.wait()


def call(kernel, outs, args, scratch=(), outer=0, room=2):
    held = [
        pltpu.with_memory_space_constraint(x, pltpu.HBM if i < outer else pltpu.VMEM)
        for i, x in enumerate(args)
    ]
    return pl.pallas_call(
        kernel,
        out_shape=outs,
        in_specs=[HB] * outer + [VM] * (len(args) - outer),
        out_specs=jax.tree.map(
            lambda o: HB if isinstance(o, jax.ShapeDtypeStruct) else VM,
            outs,
            is_leaf=lambda o: not isinstance(o, tuple),
        ),
        scratch_shapes=list(scratch),
        compiler_params=pltpu.CompilerParams(vmem_limit_bytes=room << 20),
    )(*held)


def ring(x, by):
    n = lax.axis_size("hi")
    return lax.ppermute(x, "hi", [(i, (i + by) % n) for i in range(n)])


def exchange(x):
    return lax.all_to_all(x, ("lo", "head"), split_axis=0, concat_axis=0, tiled=True)


def bf(*shape):
    return pltpu.VMEM(shape, jnp.bfloat16)


def f32(*shape):
    return pltpu.VMEM(shape, jnp.float32)


def out(*shape):
    return jax.ShapeDtypeStruct(shape, jnp.bfloat16)


def body(queries, keys, values, output_gradient, block_lo):
    rows = queries.shape[0]
    n = lax.axis_size("lo") * lax.axis_size("head")
    tok = n * rows
    blocks = tok // BLOCK
    heads = lax.axis_size("head")
    span = (WBLOCKS + 1) * BLOCK
    dma = pltpu.SemaphoreType.DMA

    kv_out, qg_out = call(
        pack_kernel,
        (bf(n, rows, 2 * HEAD_SIZE), out(n, rows + EXTRA, 4 * HEAD_SIZE)),
        (block_lo, queries, keys, values, output_gradient),
        scratch=[
            bf(EXTRA, 4 * HEAD_SIZE),
            pltpu.SMEM(block_lo.shape, jnp.int32),
            dma,
            dma((5 * n,)),
        ],
        outer=5,
    )
    kv0 = exchange(kv_out)
    kv1 = ring(kv0, 1)
    kv0, qg_out = lax.optimization_barrier((kv0, qg_out))
    qg = exchange(qg_out)
    kv2 = ring(kv1, 1)
    k_all, v_all, o, gs, p, dsf, dots, g2 = call(
        functools.partial(forward_kernel, heads),
        (
            bf(3 * tok, HEAD_SIZE),
            bf(3 * tok, HEAD_SIZE),
            bf(blocks, 2 * BLOCK, HEAD_SIZE),
            bf(blocks, 2 * BLOCK, HEAD_SIZE),
            bf(blocks, 2 * BLOCK, span),
            bf(blocks, 2 * BLOCK, tok),
            f32(blocks, 2 * BLOCK, HEAD_SIZE),
            bf(n, rows, 2 * HEAD_SIZE),
        ),
        (qg, kv0, kv1, kv2),
        scratch=[f32(tok, HEAD_SIZE), f32(tok, HEAD_SIZE)],
        room=24,
    )
    r1 = ring(g2, -1)
    od, g1, g0 = call(
        backward_kernel,
        (
            bf(n, rows, 4 * HEAD_SIZE),
            f32(n, rows, 2 * HEAD_SIZE),
            f32(n, rows, 2 * HEAD_SIZE),
        ),
        (qg, k_all, v_all, o, gs, p, dsf, dots),
        scratch=[f32(2 * tok, HEAD_SIZE), f32(2 * tok, HEAD_SIZE)],
        room=24,
    )
    od_in = exchange(od)
    t = call(add_kernel, bf(*g1.shape), (g1, r1))
    r2 = ring(t, -1)
    final = call(add_kernel, bf(*g0.shape), (g0, r2))
    g_in = exchange(final)
    return call(
        unpack_kernel,
        (out(rows, 2 * n * HEAD_SIZE),) * 2 + (out(rows, n * HEAD_SIZE),) * 2,
        (od_in, g_in),
        scratch=[dma((4 * n,))],
    )


def solution(mesh):
    seq, head = mesh.devices.shape
    kv_heads = 8
    lo = kv_heads // head
    inner = Mesh(mesh.devices.reshape(seq // lo, lo, head), ("hi", "lo", "head"))
    tokens = P(("hi", "lo", "head"), None)
    return jax.shard_map(
        body,
        mesh=inner,
        in_specs=(tokens,) * 4 + (P(("hi", "lo")),),
        out_specs=(tokens,) * 4,
        check_vma=False,
    )
```

```python
import functools

import jax
import jax.numpy as jnp
from jax import lax
from jax.experimental import pallas as pl
from jax.experimental.pallas import tpu as pltpu
from jax.sharding import Mesh, PartitionSpec as P

HEAD_SIZE = 128
BLOCK = 128
WBLOCKS = 8
LOG2E = 1.4426950408889634

query_scale = 168.0 ** (-0.5)
neg_fill = -1e30
EXTRA = 8

VM = pl.BlockSpec(memory_space=pltpu.VMEM)
HB = pl.BlockSpec(memory_space=pl.ANY)


def copy_all(pairs, sems):
    copies = [
        pltpu.make_async_copy(src, dst, sems.at[i]) for i, (src, dst) in enumerate(pairs)
    ]
    for copy in copies:
        copy.start()
    return copies


def pack_kernel(lo_ref, q_ref, k_ref, v_ref, g_ref, kv_ref, qg_ref, qg_s, lo_s, lo_sem, sems, out_sems):
    n, rows, _ = kv_ref.shape
    wide = q_ref.shape[1] // n
    fetch = pltpu.make_async_copy(lo_ref, lo_s, lo_sem)
    fetch.start()
    kv_pairs, qg_pairs = [], []
    for i in range(n):
        cols = slice(i * HEAD_SIZE, (i + 1) * HEAD_SIZE)
        kv_pairs.append((k_ref.at[:, cols], kv_ref.at[i, :, :HEAD_SIZE]))
        kv_pairs.append((v_ref.at[:, cols], kv_ref.at[i, :, HEAD_SIZE:]))
        cols = slice(i * wide, (i + 1) * wide)
        qg_pairs.append((q_ref.at[:, cols], qg_s.at[i, :rows, :wide]))
        qg_pairs.append((g_ref.at[:, cols], qg_s.at[i, :rows, wide:]))
    copies = copy_all(qg_pairs + kv_pairs, sems)
    fetch.wait()
    shards = lo_ref.shape[0]
    base = (lax.axis_index("hi") * lax.axis_size("lo") + lax.axis_index("lo")) * shards
    lane = lax.broadcasted_iota(jnp.int32, (EXTRA, 2 * wide), 1)
    told = jnp.zeros((EXTRA, 2 * wide), jnp.float32)
    for j in range(shards):
        back = (base + j - lo_s[j]).astype(jnp.float32)
        told = jnp.where(lane // BLOCK == j, back, told)
    outward = []
    for i in range(n):
        qg_s[i, rows:, :] = told.astype(jnp.bfloat16)
        copies[2 * i].wait()
        copies[2 * i + 1].wait()
        outward.append(pltpu.make_async_copy(qg_s.at[i], qg_ref.at[i], out_sems.at[i]))
        outward[i].start()
    for copy in copies[2 * n :] + outward:
        copy.wait()


def stacked(qg_ref, i, rows, first):
    per = BLOCK // rows
    return jnp.concatenate(
        [
            qg_ref[i * per : (i + 1) * per, :rows, j * HEAD_SIZE : (j + 1) * HEAD_SIZE].reshape(
                BLOCK, HEAD_SIZE
            )
            for j in (first, first + 1)
        ],
        axis=0,
    )


def nt(a, b):
    return lax.dot_general(a, b, (((1,), (1,)), ((), ())), preferred_element_type=jnp.float32)


def tn(a, b):
    return lax.dot_general(a, b, (((0,), (0,)), ((), ())), preferred_element_type=jnp.float32)


def nn(a, b):
    return jnp.dot(a, b, preferred_element_type=jnp.float32)


def forward_kernel(head_count, qg_ref, kv0_ref, kv1_ref, kv2_ref,
                   k_s, v_s, o_ref, gs_ref, p_ref, dsf_ref, dots_ref, g2_ref, dk_s, dv_s):
    n, rows, _ = kv0_ref.shape
    tok = n * rows
    blocks = tok // BLOCK
    for part, ref in enumerate((kv2_ref, kv1_ref, kv0_ref)):
        k_s[part * tok : (part + 1) * tok] = ref[:, :, :HEAD_SIZE].reshape(tok, HEAD_SIZE)
        v_s[part * tok : (part + 1) * tok] = ref[:, :, HEAD_SIZE:].reshape(tok, HEAD_SIZE)
    dk_s[...] = jnp.zeros_like(dk_s)
    dv_s[...] = jnp.zeros_like(dv_s)
    seq_blocks = head_count * rows // BLOCK
    col = lax.broadcasted_iota(jnp.int32, (2 * BLOCK, BLOCK), 1)
    row = lax.broadcasted_iota(jnp.int32, (2 * BLOCK, BLOCK), 0) % BLOCK
    hi = lax.axis_index("hi")
    scale = query_scale * LOG2E
    for i in range(blocks):
        first = 2 * tok + (i - WBLOCKS) * BLOCK
        keys = slice(first, first + (WBLOCKS + 1) * BLOCK)
        far = slice(first, tok)
        width = tok - first
        q = stacked(qg_ref, i, rows, 0)
        g = stacked(qg_ref, i, rows, 2)
        owner = (i // seq_blocks) * head_count
        lane = (i % seq_blocks) * BLOCK
        back = qg_ref[owner, rows : rows + 1, lane : lane + 1].astype(jnp.float32)
        back = jnp.minimum(back, (hi * blocks + i).astype(jnp.float32))
        s = nt(q, k_s[keys])
        parts = []
        for j in range(WBLOCKS + 1):
            part = s[:, j * BLOCK : (j + 1) * BLOCK]
            if j == WBLOCKS:
                part = jnp.where(col <= row, part, neg_fill)
            else:
                part = part + jnp.where(back < WBLOCKS - j, neg_fill, 0.0)
            if j == 0:
                part = jnp.where(col > row, part, neg_fill)
            parts.append(part)
        top = jnp.max(functools.reduce(jnp.maximum, parts), axis=1, keepdims=True)
        parts = [jnp.exp2((part - top) * scale) for part in parts]
        share = 1.0 / jnp.sum(functools.reduce(jnp.add, parts), axis=1, keepdims=True)
        e = jnp.concatenate(parts, axis=1)
        eb = e.astype(jnp.bfloat16)
        o = (nn(eb, v_s[keys]) * share).astype(jnp.bfloat16)
        dots = jnp.sum(g.astype(jnp.float32) * o.astype(jnp.float32), axis=1, keepdims=True)
        dots = dots * share
        g = (g.astype(jnp.float32) * share).astype(jnp.bfloat16)
        o_ref[i] = o
        gs_ref[i] = g
        p_ref[i, :, width:] = eb[:, width:]
        dots_ref[i] = jnp.broadcast_to(dots, (2 * BLOCK, HEAD_SIZE))
        ds = (e[:, :width] * (nt(g, v_s[far]) - dots)).astype(jnp.bfloat16)
        dsf_ref[i, :, :width] = ds
        dk_s[far] += tn(ds, q)
        dv_s[far] += tn(eb[:, :width], g)
    g2_ref[:, :, :HEAD_SIZE] = (
        (query_scale * dk_s[...]).astype(jnp.bfloat16).reshape(n, rows, HEAD_SIZE)
    )
    g2_ref[:, :, HEAD_SIZE:] = dv_s[...].astype(jnp.bfloat16).reshape(n, rows, HEAD_SIZE)


def backward_kernel(qg_ref, k_s, v_s, o_ref, gs_ref, p_ref, dsf_ref, dots_ref,
                    od_ref, g1_ref, g0_ref, dk_s, dv_s):
    n, rows, _ = od_ref.shape
    tok = n * rows
    blocks = tok // BLOCK
    per = BLOCK // rows
    dk_s[...] = jnp.zeros_like(dk_s)
    dv_s[...] = jnp.zeros_like(dv_s)
    for i in range(blocks):
        first = 2 * tok + (i - WBLOCKS) * BLOCK
        last = first + (WBLOCKS + 1) * BLOCK
        width = tok - first
        near = slice(tok, last)
        here = slice(0, last - tok)
        q = stacked(qg_ref, i, rows, 0)
        g = gs_ref[i]
        pb = p_ref[i, :, width:]
        dots = dots_ref[i, :, :1]
        ds = (pb.astype(jnp.float32) * (nt(g, v_s[near]) - dots)).astype(jnp.bfloat16)
        dq = nn(ds, k_s[near]) + nn(dsf_ref[i, :, :width], k_s[first:tok])
        dq = (query_scale * dq).astype(jnp.bfloat16)
        o = o_ref[i]
        dk_s[here] += tn(ds, q)
        dv_s[here] += tn(pb, g)
        chunk = slice(i * per, (i + 1) * per)
        for u in range(2):
            part = slice(u * BLOCK, (u + 1) * BLOCK)
            od_ref[chunk, :, u * HEAD_SIZE : (u + 1) * HEAD_SIZE] = o[part].reshape(
                per, rows, HEAD_SIZE
            )
            od_ref[chunk, :, (2 + u) * HEAD_SIZE : (3 + u) * HEAD_SIZE] = dq[part].reshape(
                per, rows, HEAD_SIZE
            )
    for part, ref in enumerate((g1_ref, g0_ref)):
        own = slice(part * tok, (part + 1) * tok)
        ref[:, :, :HEAD_SIZE] = (query_scale * dk_s[own]).reshape(n, rows, HEAD_SIZE)
        ref[:, :, HEAD_SIZE:] = dv_s[own].reshape(n, rows, HEAD_SIZE)


def add_kernel(a_ref, b_ref, o_ref):
    o_ref[...] = (a_ref[...] + b_ref[...].astype(jnp.float32)).astype(jnp.bfloat16)


def unpack_kernel(a_ref, b_ref, o_ref, dq_ref, dk_ref, dv_ref, sems):
    pairs = []
    for ref, left, right in ((a_ref, o_ref, dq_ref), (b_ref, dk_ref, dv_ref)):
        wide = ref.shape[2] // 2
        for i in range(ref.shape[0]):
            cols = slice(i * wide, (i + 1) * wide)
            pairs.append((ref.at[i, :, :wide], left.at[:, cols]))
            pairs.append((ref.at[i, :, wide:], right.at[:, cols]))
    for copy in copy_all(pairs, sems):
        copy.wait()


def call(kernel, outs, args, scratch=(), outer=0, room=2):
    held = [
        pltpu.with_memory_space_constraint(x, pltpu.HBM if i < outer else pltpu.VMEM)
        for i, x in enumerate(args)
    ]
    return pl.pallas_call(
        kernel,
        out_shape=outs,
        in_specs=[HB] * outer + [VM] * (len(args) - outer),
        out_specs=jax.tree.map(
            lambda o: HB if isinstance(o, jax.ShapeDtypeStruct) else VM,
            outs,
            is_leaf=lambda o: not isinstance(o, tuple),
        ),
        scratch_shapes=list(scratch),
        compiler_params=pltpu.CompilerParams(vmem_limit_bytes=room << 20),
    )(*held)


def ring(x, by):
    n = lax.axis_size("hi")
    return lax.ppermute(x, "hi", [(i, (i + by) % n) for i in range(n)])


def relay(x, by):
    n = lax.axis_size("hi")
    pairs = [(i, i + 1) for i in range(1, n - 1)]
    return lax.ppermute(x, "hi", pairs if by == 1 else [(j, i) for i, j in pairs])


def exchange(x):
    return lax.all_to_all(x, ("lo", "head"), split_axis=0, concat_axis=0, tiled=True)


def bf(*shape):
    return pltpu.VMEM(shape, jnp.bfloat16)


def f32(*shape):
    return pltpu.VMEM(shape, jnp.float32)


def out(*shape):
    return jax.ShapeDtypeStruct(shape, jnp.bfloat16)


def body(queries, keys, values, output_gradient, block_lo):
    rows = queries.shape[0]
    n = lax.axis_size("lo") * lax.axis_size("head")
    tok = n * rows
    blocks = tok // BLOCK
    heads = lax.axis_size("head")
    span = (WBLOCKS + 1) * BLOCK
    dma = pltpu.SemaphoreType.DMA

    kv_out, qg_out = call(
        pack_kernel,
        (bf(n, rows, 2 * HEAD_SIZE), out(n, rows + EXTRA, 4 * HEAD_SIZE)),
        (block_lo, queries, keys, values, output_gradient),
        scratch=[
            bf(n, rows + EXTRA, 4 * HEAD_SIZE),
            pltpu.SMEM(block_lo.shape, jnp.int32),
            dma,
            dma((4 * n,)),
            dma((n,)),
        ],
        outer=5,
    )
    kv0 = exchange(kv_out)
    kv1 = ring(kv0, 1)
    kv0, qg_out = lax.optimization_barrier((kv0, qg_out))
    qg = exchange(qg_out)
    kv2 = relay(kv1, 1)
    k_all, v_all, o, gs, p, dsf, dots, g2 = call(
        functools.partial(forward_kernel, heads),
        (
            bf(3 * tok, HEAD_SIZE),
            bf(3 * tok, HEAD_SIZE),
            bf(blocks, 2 * BLOCK, HEAD_SIZE),
            bf(blocks, 2 * BLOCK, HEAD_SIZE),
            bf(blocks, 2 * BLOCK, span),
            bf(blocks, 2 * BLOCK, tok),
            f32(blocks, 2 * BLOCK, HEAD_SIZE),
            bf(n, rows, 2 * HEAD_SIZE),
        ),
        (qg, kv0, kv1, kv2),
        scratch=[f32(tok, HEAD_SIZE), f32(tok, HEAD_SIZE)],
        room=24,
    )
    r1 = relay(g2, -1)
    od, g1, g0 = call(
        backward_kernel,
        (
            bf(n, rows, 4 * HEAD_SIZE),
            f32(n, rows, 2 * HEAD_SIZE),
            f32(n, rows, 2 * HEAD_SIZE),
        ),
        (qg, k_all, v_all, o, gs, p, dsf, dots),
        scratch=[f32(2 * tok, HEAD_SIZE), f32(2 * tok, HEAD_SIZE)],
        room=24,
    )
    od_in = exchange(od)
    t = call(add_kernel, bf(*g1.shape), (g1, r1))
    r2 = ring(t, -1)
    final = call(add_kernel, bf(*g0.shape), (g0, r2))
    g_in = exchange(final)
    return call(
        unpack_kernel,
        (out(rows, 2 * n * HEAD_SIZE),) * 2 + (out(rows, n * HEAD_SIZE),) * 2,
        (od_in, g_in),
        scratch=[dma((4 * n,))],
    )


def solution(mesh):
    seq, head = mesh.devices.shape
    kv_heads = 8
    lo = kv_heads // head
    inner = Mesh(mesh.devices.reshape(seq // lo, lo, head), ("hi", "lo", "head"))
    tokens = P(("hi", "lo", "head"), None)
    return jax.shard_map(
        body,
        mesh=inner,
        in_specs=(tokens,) * 4 + (P(("hi", "lo")),),
        out_specs=(tokens,) * 4,
        check_vma=False,
    )
```

```python
import functools

import jax
import jax.numpy as jnp
from jax import lax
from jax.experimental import pallas as pl
from jax.experimental.pallas import tpu as pltpu
from jax.sharding import Mesh, PartitionSpec as P

HEAD_SIZE = 128
BLOCK = 128
WBLOCKS = 8
LOG2E = 1.4426950408889634

query_scale = 168.0 ** (-0.5)
neg_fill = -1e30
EXTRA = 8

VM = pl.BlockSpec(memory_space=pltpu.VMEM)
HB = pl.BlockSpec(memory_space=pl.ANY)


def copy_all(pairs, sems):
    copies = [
        pltpu.make_async_copy(src, dst, sems.at[i]) for i, (src, dst) in enumerate(pairs)
    ]
    for copy in copies:
        copy.start()
    return copies


def pack_kernel(lo_ref, q_ref, k_ref, v_ref, g_ref, kv_ref, qg_ref, qg_s, lo_s, lo_sem, sems, out_sems):
    n, rows, _ = kv_ref.shape
    wide = q_ref.shape[1] // n
    fetch = pltpu.make_async_copy(lo_ref, lo_s, lo_sem)
    fetch.start()
    kv_pairs, qg_pairs = [], []
    for i in range(n):
        cols = slice(i * HEAD_SIZE, (i + 1) * HEAD_SIZE)
        kv_pairs.append((k_ref.at[:, cols], kv_ref.at[i, :, :HEAD_SIZE]))
        kv_pairs.append((v_ref.at[:, cols], kv_ref.at[i, :, HEAD_SIZE:]))
        cols = slice(i * wide, (i + 1) * wide)
        qg_pairs.append((q_ref.at[:, cols], qg_s.at[i, :rows, :wide]))
        qg_pairs.append((g_ref.at[:, cols], qg_s.at[i, :rows, wide:]))
    copies = copy_all(qg_pairs + kv_pairs, sems)
    fetch.wait()
    shards = lo_ref.shape[0]
    base = (lax.axis_index("hi") * lax.axis_size("lo") + lax.axis_index("lo")) * shards
    lane = lax.broadcasted_iota(jnp.int32, (EXTRA, 2 * wide), 1)
    told = jnp.zeros((EXTRA, 2 * wide), jnp.float32)
    for j in range(shards):
        back = (base + j - lo_s[j]).astype(jnp.float32)
        told = jnp.where(lane // BLOCK == j, back, told)
    outward = []
    for i in range(n):
        qg_s[i, rows:, :] = told.astype(jnp.bfloat16)
        copies[2 * i].wait()
        copies[2 * i + 1].wait()
        outward.append(pltpu.make_async_copy(qg_s.at[i], qg_ref.at[i], out_sems.at[i]))
        outward[i].start()
    for copy in copies[2 * n :] + outward:
        copy.wait()


def stacked(qg_ref, i, rows, first):
    per = BLOCK // rows
    return jnp.concatenate(
        [
            qg_ref[i * per : (i + 1) * per, :rows, j * HEAD_SIZE : (j + 1) * HEAD_SIZE].reshape(
                BLOCK, HEAD_SIZE
            )
            for j in (first, first + 1)
        ],
        axis=0,
    )


def nt(a, b):
    return lax.dot_general(a, b, (((1,), (1,)), ((), ())), preferred_element_type=jnp.float32)


def tn(a, b):
    return lax.dot_general(a, b, (((0,), (0,)), ((), ())), preferred_element_type=jnp.float32)


def nn(a, b):
    return jnp.dot(a, b, preferred_element_type=jnp.float32)


def spread(a, b):
    lane = lax.broadcasted_iota(jnp.int32, (a.shape[0], HEAD_SIZE), 1)
    return jnp.where(lane < HEAD_SIZE // 2, a, b)


def softmax_parts(s, cols, back, scale):
    col = lax.broadcasted_iota(jnp.int32, (2 * BLOCK, BLOCK), 1)
    row = lax.broadcasted_iota(jnp.int32, (2 * BLOCK, BLOCK), 0) % BLOCK
    parts = []
    for at, j in enumerate(cols):
        part = s[:, at * BLOCK : (at + 1) * BLOCK]
        if j == WBLOCKS:
            part = jnp.where(col <= row, part, neg_fill)
        else:
            part = part + jnp.where(back < WBLOCKS - j, neg_fill, 0.0)
        if j == 0:
            part = jnp.where(col > row, part, neg_fill)
        parts.append(part)
    top = jnp.max(functools.reduce(jnp.maximum, parts), axis=1, keepdims=True)
    parts = [jnp.exp2((part - top) * scale) for part in parts]
    total = jnp.sum(functools.reduce(jnp.add, parts), axis=1, keepdims=True)
    return jnp.concatenate(parts, axis=1), top, total


def blocks_back(qg_ref, i, rows, head_count):
    blocks = qg_ref.shape[0] * rows // BLOCK
    seq_blocks = head_count * rows // BLOCK
    owner = (i // seq_blocks) * head_count
    lane = (i % seq_blocks) * BLOCK
    back = qg_ref[owner, rows : rows + 1, lane : lane + 1].astype(jnp.float32)
    return jnp.minimum(back, (lax.axis_index("hi") * blocks + i).astype(jnp.float32))


def near_kernel(head_count, qg_ref, kv0_ref, kv1_ref, k_s, v_s, o_ref, p_ref, stat_ref):
    n, rows, _ = kv0_ref.shape
    tok = n * rows
    blocks = tok // BLOCK
    for part, ref in enumerate((kv1_ref, kv0_ref)):
        k_s[part * tok : (part + 1) * tok] = ref[:, :, :HEAD_SIZE].reshape(tok, HEAD_SIZE)
        v_s[part * tok : (part + 1) * tok] = ref[:, :, HEAD_SIZE:].reshape(tok, HEAD_SIZE)

    def step(i, start):
        keys = slice(start, tok + (i + 1) * BLOCK)
        count = keys.stop // BLOCK - start // BLOCK
        back = blocks_back(qg_ref, i, rows, head_count)
        s = nt(stacked(qg_ref, i, rows, 0), k_s[keys])
        e, top, total = softmax_parts(
            s, range(WBLOCKS + 1 - count, WBLOCKS + 1), back, query_scale * LOG2E
        )
        eb = e.astype(jnp.bfloat16)
        o_ref[i] = nn(eb, v_s[keys])
        p_ref[i, :, keys] = eb
        stat_ref[i] = spread(top, total)

    hi = lax.axis_index("hi")

    @pl.when(hi == 0)
    def _():
        for i in range(blocks):
            step(i, tok)

    @pl.when(hi > 0)
    def _():
        for i in range(blocks):
            step(i, 0)


def far_kernel(head_count, qg_ref, kv2_ref, near_ref, stat_ref,
               k_s, o_ref, gs_ref, dsf_ref, dots_ref, g2_ref, v_s, dk_s, dv_s):
    n, rows, _ = kv2_ref.shape
    tok = n * rows
    blocks = tok // BLOCK
    scale = query_scale * LOG2E

    def step(i, far_seen):
        q = stacked(qg_ref, i, rows, 0)
        g = stacked(qg_ref, i, rows, 2).astype(jnp.float32)
        top = stat_ref[i, :, :1]
        total = stat_ref[i, :, HEAD_SIZE // 2 : HEAD_SIZE // 2 + 1]
        if far_seen:
            far = slice(i * BLOCK, tok)
            width = tok - i * BLOCK
            back = blocks_back(qg_ref, i, rows, head_count)
            s = nt(q, k_s[far])
            e, far_top, far_total = softmax_parts(s, range(width // BLOCK), back, scale)
            eb = e.astype(jnp.bfloat16)
            most = jnp.maximum(top, far_top)
            near = jnp.exp2((top - most) * scale)
            away = jnp.exp2((far_top - most) * scale)
            share = 1.0 / (near * total + away * far_total)
            near = near * share
            away = away * share
            o = near_ref[i] * near + nn(eb, v_s[far]) * away
        else:
            near = 1.0 / total
            o = near_ref[i] * near
        o = o.astype(jnp.bfloat16)
        dots = jnp.sum(g * o.astype(jnp.float32), axis=1, keepdims=True)
        o_ref[i] = o
        gs_ref[i] = (g * near).astype(jnp.bfloat16)
        dots_ref[i] = jnp.broadcast_to(dots * near, (2 * BLOCK, HEAD_SIZE))
        if far_seen:
            g = (g * away).astype(jnp.bfloat16)
            ds = (e * (nt(g, v_s[far]) - dots * away)).astype(jnp.bfloat16)
            dsf_ref[i, :, :width] = ds
            dk_s[far] += tn(ds, q)
            dv_s[far] += tn(eb, g)

    hi = lax.axis_index("hi")

    @pl.when(hi == 0)
    def _():
        for i in range(blocks):
            step(i, False)
        g2_ref[...] = jnp.zeros_like(g2_ref)

    @pl.when(hi > 0)
    def _():
        k_s[...] = kv2_ref[:, :, :HEAD_SIZE].reshape(tok, HEAD_SIZE)
        v_s[...] = kv2_ref[:, :, HEAD_SIZE:].reshape(tok, HEAD_SIZE)
        dk_s[...] = jnp.zeros_like(dk_s)
        dv_s[...] = jnp.zeros_like(dv_s)
        for i in range(blocks):
            step(i, True)
        g2_ref[:, :, :HEAD_SIZE] = (
            (query_scale * dk_s[...]).astype(jnp.bfloat16).reshape(n, rows, HEAD_SIZE)
        )
        g2_ref[:, :, HEAD_SIZE:] = dv_s[...].astype(jnp.bfloat16).reshape(n, rows, HEAD_SIZE)


def backward_kernel(qg_ref, k_s, v_s, kf_ref, o_ref, gs_ref, p_ref, dsf_ref, dots_ref,
                    od_ref, g1_ref, g0_ref, dk_s, dv_s):
    n, rows, _ = od_ref.shape
    tok = n * rows
    blocks = tok // BLOCK
    per = BLOCK // rows
    dk_s[...] = jnp.zeros_like(dk_s)
    dv_s[...] = jnp.zeros_like(dv_s)

    def step(i, own_only):
        near = slice(tok if own_only else 0, tok + (i + 1) * BLOCK)
        q = stacked(qg_ref, i, rows, 0)
        g = gs_ref[i]
        pb = p_ref[i, :, near]
        dots = dots_ref[i, :, :1]
        ds = (pb.astype(jnp.float32) * (nt(g, v_s[near]) - dots)).astype(jnp.bfloat16)
        dq = nn(ds, k_s[near])
        if not own_only:
            dq = dq + nn(dsf_ref[i, :, : tok - i * BLOCK], kf_ref[i * BLOCK :])
        dq = (query_scale * dq).astype(jnp.bfloat16)
        o = o_ref[i]
        dk_s[near] += tn(ds, q)
        dv_s[near] += tn(pb, g)
        chunk = slice(i * per, (i + 1) * per)
        for u in range(2):
            part = slice(u * BLOCK, (u + 1) * BLOCK)
            od_ref[chunk, :, u * HEAD_SIZE : (u + 1) * HEAD_SIZE] = o[part].reshape(
                per, rows, HEAD_SIZE
            )
            od_ref[chunk, :, (2 + u) * HEAD_SIZE : (3 + u) * HEAD_SIZE] = dq[part].reshape(
                per, rows, HEAD_SIZE
            )

    hi = lax.axis_index("hi")

    @pl.when(hi == 0)
    def _():
        for i in range(blocks):
            step(i, True)

    @pl.when(hi > 0)
    def _():
        for i in range(blocks):
            step(i, False)

    for part, ref in enumerate((g1_ref, g0_ref)):
        own = slice(part * tok, (part + 1) * tok)
        ref[:, :, :HEAD_SIZE] = (query_scale * dk_s[own]).reshape(n, rows, HEAD_SIZE)
        ref[:, :, HEAD_SIZE:] = dv_s[own].reshape(n, rows, HEAD_SIZE)


def add_kernel(a_ref, b_ref, o_ref):
    o_ref[...] = (a_ref[...] + b_ref[...].astype(jnp.float32)).astype(jnp.bfloat16)


def unpack_kernel(a_ref, b_ref, o_ref, dq_ref, dk_ref, dv_ref, sems):
    pairs = []
    for ref, left, right in ((a_ref, o_ref, dq_ref), (b_ref, dk_ref, dv_ref)):
        wide = ref.shape[2] // 2
        for i in range(ref.shape[0]):
            cols = slice(i * wide, (i + 1) * wide)
            pairs.append((ref.at[i, :, :wide], left.at[:, cols]))
            pairs.append((ref.at[i, :, wide:], right.at[:, cols]))
    for copy in copy_all(pairs, sems):
        copy.wait()


def call(kernel, outs, args, scratch=(), outer=0, room=2):
    held = [
        pltpu.with_memory_space_constraint(x, pltpu.HBM if i < outer else pltpu.VMEM)
        for i, x in enumerate(args)
    ]
    return pl.pallas_call(
        kernel,
        out_shape=outs,
        in_specs=[HB] * outer + [VM] * (len(args) - outer),
        out_specs=jax.tree.map(
            lambda o: HB if isinstance(o, jax.ShapeDtypeStruct) else VM,
            outs,
            is_leaf=lambda o: not isinstance(o, tuple),
        ),
        scratch_shapes=list(scratch),
        compiler_params=pltpu.CompilerParams(vmem_limit_bytes=room << 20),
    )(*held)


def ring(x, by):
    n = lax.axis_size("hi")
    return lax.ppermute(x, "hi", [(i, (i + by) % n) for i in range(n)])


def relay(x):
    n = lax.axis_size("hi")
    return lax.ppermute(x, "hi", [(i, i + 1) for i in range(1, n - 1)])


def exchange(x):
    return lax.all_to_all(x, ("lo", "head"), split_axis=0, concat_axis=0, tiled=True)


def bf(*shape):
    return pltpu.VMEM(shape, jnp.bfloat16)


def f32(*shape):
    return pltpu.VMEM(shape, jnp.float32)


def out(*shape):
    return jax.ShapeDtypeStruct(shape, jnp.bfloat16)


def body(queries, keys, values, output_gradient, block_lo):
    rows = queries.shape[0]
    n = lax.axis_size("lo") * lax.axis_size("head")
    tok = n * rows
    blocks = tok // BLOCK
    heads = lax.axis_size("head")
    dma = pltpu.SemaphoreType.DMA

    kv_out, qg_out = call(
        pack_kernel,
        (bf(n, rows, 2 * HEAD_SIZE), out(n, rows + EXTRA, 4 * HEAD_SIZE)),
        (block_lo, queries, keys, values, output_gradient),
        scratch=[
            bf(n, rows + EXTRA, 4 * HEAD_SIZE),
            pltpu.SMEM(block_lo.shape, jnp.int32),
            dma,
            dma((4 * n,)),
            dma((n,)),
        ],
        outer=5,
    )
    kv0 = exchange(kv_out)
    kv1 = ring(kv0, 1)
    kv0, qg_out = lax.optimization_barrier((kv0, qg_out))
    qg = exchange(qg_out)
    kv2 = relay(kv1)
    k_all, v_all, near, p, stat = call(
        functools.partial(near_kernel, heads),
        (
            bf(2 * tok, HEAD_SIZE),
            bf(2 * tok, HEAD_SIZE),
            f32(blocks, 2 * BLOCK, HEAD_SIZE),
            bf(blocks, 2 * BLOCK, 2 * tok),
            f32(blocks, 2 * BLOCK, HEAD_SIZE),
        ),
        (qg, kv0, kv1),
        room=20,
    )
    k_far, o, gs, dsf, dots, g2 = call(
        functools.partial(far_kernel, heads),
        (
            bf(tok, HEAD_SIZE),
            bf(blocks, 2 * BLOCK, HEAD_SIZE),
            bf(blocks, 2 * BLOCK, HEAD_SIZE),
            bf(blocks, 2 * BLOCK, tok),
            f32(blocks, 2 * BLOCK, HEAD_SIZE),
            bf(n, rows, 2 * HEAD_SIZE),
        ),
        (qg, kv2, near, stat),
        scratch=[bf(tok, HEAD_SIZE), f32(tok, HEAD_SIZE), f32(tok, HEAD_SIZE)],
        room=20,
    )
    r1 = ring(g2, -1)
    od, g1, g0 = call(
        backward_kernel,
        (
            bf(n, rows, 4 * HEAD_SIZE),
            f32(n, rows, 2 * HEAD_SIZE),
            f32(n, rows, 2 * HEAD_SIZE),
        ),
        (qg, k_all, v_all, k_far, o, gs, p, dsf, dots),
        scratch=[f32(2 * tok, HEAD_SIZE), f32(2 * tok, HEAD_SIZE)],
        room=24,
    )
    od_in = exchange(od)
    t = call(add_kernel, bf(*g1.shape), (g1, r1))
    r2 = ring(t, -1)
    final = call(add_kernel, bf(*g0.shape), (g0, r2))
    g_in = exchange(final)
    return call(
        unpack_kernel,
        (out(rows, 2 * n * HEAD_SIZE),) * 2 + (out(rows, n * HEAD_SIZE),) * 2,
        (od_in, g_in),
        scratch=[dma((4 * n,))],
    )


def solution(mesh):
    seq, head = mesh.devices.shape
    kv_heads = 8
    lo = kv_heads // head
    inner = Mesh(mesh.devices.reshape(seq // lo, lo, head), ("hi", "lo", "head"))
    tokens = P(("hi", "lo", "head"), None)
    return jax.shard_map(
        body,
        mesh=inner,
        in_specs=(tokens,) * 4 + (P(("hi", "lo")),),
        out_specs=(tokens,) * 4,
        check_vma=False,
    )
```

```python
import functools

import jax
import jax.numpy as jnp
from jax import lax
from jax.experimental import pallas as pl
from jax.experimental.pallas import tpu as pltpu
from jax.sharding import Mesh, PartitionSpec as P

HEAD_SIZE = 128
BLOCK = 128
WBLOCKS = 8
LOG2E = 1.4426950408889634

query_scale = 168.0 ** (-0.5)
neg_fill = -1e30
EXTRA = 8

VM = pl.BlockSpec(memory_space=pltpu.VMEM)
HB = pl.BlockSpec(memory_space=pl.ANY)


def copy_all(pairs, sems):
    copies = [
        pltpu.make_async_copy(src, dst, sems.at[i]) for i, (src, dst) in enumerate(pairs)
    ]
    for copy in copies:
        copy.start()
    return copies


def pack_kernel(lo_ref, q_ref, k_ref, v_ref, g_ref, kv_ref, qg_ref, qg_s, lo_s, lo_sem, sems, out_sems):
    n, rows, _ = kv_ref.shape
    wide = q_ref.shape[1] // n
    fetch = pltpu.make_async_copy(lo_ref, lo_s, lo_sem)
    fetch.start()
    kv_pairs, qg_pairs = [], []
    for i in range(n):
        cols = slice(i * HEAD_SIZE, (i + 1) * HEAD_SIZE)
        kv_pairs.append((k_ref.at[:, cols], kv_ref.at[i, :, :HEAD_SIZE]))
        kv_pairs.append((v_ref.at[:, cols], kv_ref.at[i, :, HEAD_SIZE:]))
        cols = slice(i * wide, (i + 1) * wide)
        qg_pairs.append((q_ref.at[:, cols], qg_s.at[i, :rows, :wide]))
        qg_pairs.append((g_ref.at[:, cols], qg_s.at[i, :rows, wide:]))
    copies = copy_all(qg_pairs + kv_pairs, sems)
    fetch.wait()
    shards = lo_ref.shape[0]
    base = (lax.axis_index("hi") * lax.axis_size("lo") + lax.axis_index("lo")) * shards
    lane = lax.broadcasted_iota(jnp.int32, (EXTRA, 2 * wide), 1)
    told = jnp.zeros((EXTRA, 2 * wide), jnp.float32)
    for j in range(shards):
        back = (base + j - lo_s[j]).astype(jnp.float32)
        told = jnp.where(lane // BLOCK == j, back, told)
    outward = []
    for i in range(n):
        qg_s[i, rows:, :] = told.astype(jnp.bfloat16)
        copies[2 * i].wait()
        copies[2 * i + 1].wait()
        outward.append(pltpu.make_async_copy(qg_s.at[i], qg_ref.at[i], out_sems.at[i]))
        outward[i].start()
    for copy in copies[2 * n :] + outward:
        copy.wait()


def stacked(qg_ref, i, rows, first):
    per = BLOCK // rows
    return jnp.concatenate(
        [
            qg_ref[i * per : (i + 1) * per, :rows, j * HEAD_SIZE : (j + 1) * HEAD_SIZE].reshape(
                BLOCK, HEAD_SIZE
            )
            for j in (first, first + 1)
        ],
        axis=0,
    )


def nt(a, b):
    return lax.dot_general(a, b, (((1,), (1,)), ((), ())), preferred_element_type=jnp.float32)


def tn(a, b):
    return lax.dot_general(a, b, (((0,), (0,)), ((), ())), preferred_element_type=jnp.float32)


def nn(a, b):
    return jnp.dot(a, b, preferred_element_type=jnp.float32)


def spread(a, b):
    lane = lax.broadcasted_iota(jnp.int32, (a.shape[0], HEAD_SIZE), 1)
    return jnp.where(lane < HEAD_SIZE // 2, a, b)


def softmax_parts(s, cols, back, scale):
    col = lax.broadcasted_iota(jnp.int32, (2 * BLOCK, BLOCK), 1)
    row = lax.broadcasted_iota(jnp.int32, (2 * BLOCK, BLOCK), 0) % BLOCK
    parts = []
    for at, j in enumerate(cols):
        part = s[:, at * BLOCK : (at + 1) * BLOCK]
        if j == WBLOCKS:
            part = jnp.where(col <= row, part, neg_fill)
        else:
            part = part + jnp.where(back < WBLOCKS - j, neg_fill, 0.0)
        if j == 0:
            part = jnp.where(col > row, part, neg_fill)
        parts.append(part)
    top = jnp.max(functools.reduce(jnp.maximum, parts), axis=1, keepdims=True)
    parts = [jnp.exp2((part - top) * scale) for part in parts]
    total = jnp.sum(functools.reduce(jnp.add, parts), axis=1, keepdims=True)
    return jnp.concatenate(parts, axis=1), top, total


def blocks_back(qg_ref, i, rows, head_count):
    blocks = qg_ref.shape[0] * rows // BLOCK
    seq_blocks = head_count * rows // BLOCK
    owner = (i // seq_blocks) * head_count
    lane = (i % seq_blocks) * BLOCK
    back = qg_ref[owner, rows : rows + 1, lane : lane + 1].astype(jnp.float32)
    return jnp.minimum(back, (lax.axis_index("hi") * blocks + i).astype(jnp.float32))


def near_kernel(head_count, qg_ref, kv0_ref, kv1_ref, k_s, v_s, o_ref, p_ref, stat_ref):
    n, rows, _ = kv0_ref.shape
    tok = n * rows
    blocks = tok // BLOCK
    for part, ref in enumerate((kv1_ref, kv0_ref)):
        k_s[part * tok : (part + 1) * tok] = ref[:, :, :HEAD_SIZE].reshape(tok, HEAD_SIZE)
        v_s[part * tok : (part + 1) * tok] = ref[:, :, HEAD_SIZE:].reshape(tok, HEAD_SIZE)

    def step(i, start):
        keys = slice(start, tok + (i + 1) * BLOCK)
        count = keys.stop // BLOCK - start // BLOCK
        back = blocks_back(qg_ref, i, rows, head_count)
        s = nt(stacked(qg_ref, i, rows, 0), k_s[keys])
        e, top, total = softmax_parts(
            s, range(WBLOCKS + 1 - count, WBLOCKS + 1), back, query_scale * LOG2E
        )
        eb = e.astype(jnp.bfloat16)
        o_ref[i] = nn(eb, v_s[keys])
        p_ref[i, :, keys] = eb
        stat_ref[i] = spread(top, total)

    hi = lax.axis_index("hi")

    @pl.when(hi == 0)
    def _():
        for i in range(blocks):
            step(i, tok)

    @pl.when(hi > 0)
    def _():
        for i in range(blocks):
            step(i, 0)


def far_kernel(head_count, qg_ref, kv2_ref, near_ref, stat_ref,
               k_s, o_ref, gs_ref, dsf_ref, dots_ref, g2_ref, v_s, dk_s, dv_s):
    n, rows, _ = kv2_ref.shape
    tok = n * rows
    blocks = tok // BLOCK
    scale = query_scale * LOG2E

    def step(i, far_seen):
        q = stacked(qg_ref, i, rows, 0)
        g = stacked(qg_ref, i, rows, 2).astype(jnp.float32)
        top = stat_ref[i, :, :1]
        total = stat_ref[i, :, HEAD_SIZE // 2 : HEAD_SIZE // 2 + 1]
        if far_seen:
            far = slice(i * BLOCK, tok)
            width = tok - i * BLOCK
            back = blocks_back(qg_ref, i, rows, head_count)
            s = nt(q, k_s[far])
            e, far_top, far_total = softmax_parts(s, range(width // BLOCK), back, scale)
            eb = e.astype(jnp.bfloat16)
            most = jnp.maximum(top, far_top)
            near = jnp.exp2((top - most) * scale)
            away = jnp.exp2((far_top - most) * scale)
            share = 1.0 / (near * total + away * far_total)
            near = near * share
            away = away * share
            o = near_ref[i] * near + nn(eb, v_s[far]) * away
        else:
            near = 1.0 / total
            o = near_ref[i] * near
        o = o.astype(jnp.bfloat16)
        dots = jnp.sum(g * o.astype(jnp.float32), axis=1, keepdims=True)
        o_ref[i] = o
        gs_ref[i] = (g * near).astype(jnp.bfloat16)
        dots_ref[i] = jnp.broadcast_to(dots * near, (2 * BLOCK, HEAD_SIZE))
        if far_seen:
            g = (g * away).astype(jnp.bfloat16)
            ds = (e * (nt(g, v_s[far]) - dots * away)).astype(jnp.bfloat16)
            dsf_ref[i, :, :width] = ds
            dk_s[far] += tn(ds, q)
            dv_s[far] += tn(eb, g)

    hi = lax.axis_index("hi")

    @pl.when(hi == 0)
    def _():
        for i in range(blocks):
            step(i, False)
        g2_ref[...] = jnp.zeros_like(g2_ref)

    @pl.when(hi > 0)
    def _():
        k_s[...] = kv2_ref[:, :, :HEAD_SIZE].reshape(tok, HEAD_SIZE)
        v_s[...] = kv2_ref[:, :, HEAD_SIZE:].reshape(tok, HEAD_SIZE)
        dk_s[...] = jnp.zeros_like(dk_s)
        dv_s[...] = jnp.zeros_like(dv_s)
        for i in range(blocks):
            step(i, True)
        g2_ref[:, :, :HEAD_SIZE] = (
            (query_scale * dk_s[...]).astype(jnp.bfloat16).reshape(n, rows, HEAD_SIZE)
        )
        g2_ref[:, :, HEAD_SIZE:] = dv_s[...].astype(jnp.bfloat16).reshape(n, rows, HEAD_SIZE)


def backward_kernel(qg_ref, k_s, v_s, kf_ref, o_ref, gs_ref, p_ref, dsf_ref, dots_ref,
                    od_ref, g1_ref, g0_ref, dk_s, dv_s):
    n, rows, _ = od_ref.shape
    tok = n * rows
    blocks = tok // BLOCK
    per = BLOCK // rows
    dk_s[...] = jnp.zeros_like(dk_s)
    dv_s[...] = jnp.zeros_like(dv_s)

    def step(i, own_only):
        near = slice(tok if own_only else 0, tok + (i + 1) * BLOCK)
        q = stacked(qg_ref, i, rows, 0)
        g = gs_ref[i]
        pb = p_ref[i, :, near]
        dots = dots_ref[i, :, :1]
        ds = (pb.astype(jnp.float32) * (nt(g, v_s[near]) - dots)).astype(jnp.bfloat16)
        dq = nn(ds, k_s[near])
        if not own_only:
            dq = dq + nn(dsf_ref[i, :, : tok - i * BLOCK], kf_ref[i * BLOCK :])
        dq = (query_scale * dq).astype(jnp.bfloat16)
        o = o_ref[i]
        dk_s[near] += tn(ds, q)
        dv_s[near] += tn(pb, g)
        chunk = slice(i * per, (i + 1) * per)
        for u in range(2):
            part = slice(u * BLOCK, (u + 1) * BLOCK)
            od_ref[chunk, :, u * HEAD_SIZE : (u + 1) * HEAD_SIZE] = o[part].reshape(
                per, rows, HEAD_SIZE
            )
            od_ref[chunk, :, (2 + u) * HEAD_SIZE : (3 + u) * HEAD_SIZE] = dq[part].reshape(
                per, rows, HEAD_SIZE
            )

    hi = lax.axis_index("hi")

    @pl.when(hi == 0)
    def _():
        for i in range(blocks):
            step(i, True)

    @pl.when(hi > 0)
    def _():
        for i in range(blocks):
            step(i, False)

    for part, ref in enumerate((g1_ref, g0_ref)):
        own = slice(part * tok, (part + 1) * tok)
        ref[:, :, :HEAD_SIZE] = (query_scale * dk_s[own]).reshape(n, rows, HEAD_SIZE)
        ref[:, :, HEAD_SIZE:] = dv_s[own].reshape(n, rows, HEAD_SIZE)


def add_kernel(a_ref, b_ref, o_ref):
    o_ref[...] = (a_ref[...] + b_ref[...].astype(jnp.float32)).astype(jnp.bfloat16)


def unpack_kernel(a_ref, b_ref, o_ref, dq_ref, dk_ref, dv_ref, sems):
    pairs = []
    for ref, left, right in ((a_ref, o_ref, dq_ref), (b_ref, dk_ref, dv_ref)):
        wide = ref.shape[2] // 2
        for i in range(ref.shape[0]):
            cols = slice(i * wide, (i + 1) * wide)
            pairs.append((ref.at[i, :, :wide], left.at[:, cols]))
            pairs.append((ref.at[i, :, wide:], right.at[:, cols]))
    for copy in copy_all(pairs, sems):
        copy.wait()


def call(kernel, outs, args, scratch=(), outer=0, room=2):
    held = [
        pltpu.with_memory_space_constraint(x, pltpu.HBM if i < outer else pltpu.VMEM)
        for i, x in enumerate(args)
    ]
    return pl.pallas_call(
        kernel,
        out_shape=outs,
        in_specs=[HB] * outer + [VM] * (len(args) - outer),
        out_specs=jax.tree.map(
            lambda o: HB if isinstance(o, jax.ShapeDtypeStruct) else VM,
            outs,
            is_leaf=lambda o: not isinstance(o, tuple),
        ),
        scratch_shapes=list(scratch),
        compiler_params=pltpu.CompilerParams(vmem_limit_bytes=room << 20),
    )(*held)


def ring(x, by):
    n = lax.axis_size("hi")
    return lax.ppermute(x, "hi", [(i, (i + by) % n) for i in range(n)])


def line(x, by, least=0):
    n = lax.axis_size("hi")
    pairs = [(i, i + 1) for i in range(least, n - 1)]
    return lax.ppermute(x, "hi", pairs if by == 1 else [(j, i) for i, j in pairs])


def exchange(x):
    return lax.all_to_all(x, ("lo", "head"), split_axis=0, concat_axis=0, tiled=True)


def bf(*shape):
    return pltpu.VMEM(shape, jnp.bfloat16)


def f32(*shape):
    return pltpu.VMEM(shape, jnp.float32)


def out(*shape):
    return jax.ShapeDtypeStruct(shape, jnp.bfloat16)


def body(queries, keys, values, output_gradient, block_lo):
    rows = queries.shape[0]
    n = lax.axis_size("lo") * lax.axis_size("head")
    tok = n * rows
    blocks = tok // BLOCK
    heads = lax.axis_size("head")
    dma = pltpu.SemaphoreType.DMA

    kv_out, qg_out = call(
        pack_kernel,
        (bf(n, rows, 2 * HEAD_SIZE), out(n, rows + EXTRA, 4 * HEAD_SIZE)),
        (block_lo, queries, keys, values, output_gradient),
        scratch=[
            bf(n, rows + EXTRA, 4 * HEAD_SIZE),
            pltpu.SMEM(block_lo.shape, jnp.int32),
            dma,
            dma((4 * n,)),
            dma((n,)),
        ],
        outer=5,
    )
    kv0 = exchange(kv_out)
    kv1 = ring(kv0, 1)
    kv0, qg_out = lax.optimization_barrier((kv0, qg_out))
    qg = exchange(qg_out)
    kv2 = line(kv1, 1, 1)
    k_all, v_all, near, p, stat = call(
        functools.partial(near_kernel, heads),
        (
            bf(2 * tok, HEAD_SIZE),
            bf(2 * tok, HEAD_SIZE),
            f32(blocks, 2 * BLOCK, HEAD_SIZE),
            bf(blocks, 2 * BLOCK, 2 * tok),
            f32(blocks, 2 * BLOCK, HEAD_SIZE),
        ),
        (qg, kv0, kv1),
        room=20,
    )
    k_far, o, gs, dsf, dots, g2 = call(
        functools.partial(far_kernel, heads),
        (
            bf(tok, HEAD_SIZE),
            bf(blocks, 2 * BLOCK, HEAD_SIZE),
            bf(blocks, 2 * BLOCK, HEAD_SIZE),
            bf(blocks, 2 * BLOCK, tok),
            f32(blocks, 2 * BLOCK, HEAD_SIZE),
            bf(n, rows, 2 * HEAD_SIZE),
        ),
        (qg, kv2, near, stat),
        scratch=[bf(tok, HEAD_SIZE), f32(tok, HEAD_SIZE), f32(tok, HEAD_SIZE)],
        room=20,
    )
    r1 = line(g2, -1, 1)
    od, g1, g0 = call(
        backward_kernel,
        (
            bf(n, rows, 4 * HEAD_SIZE),
            f32(n, rows, 2 * HEAD_SIZE),
            f32(n, rows, 2 * HEAD_SIZE),
        ),
        (qg, k_all, v_all, k_far, o, gs, p, dsf, dots),
        scratch=[f32(2 * tok, HEAD_SIZE), f32(2 * tok, HEAD_SIZE)],
        room=24,
    )
    od_in = exchange(od)
    t = call(add_kernel, bf(*g1.shape), (g1, r1))
    r2 = line(t, -1)
    final = call(add_kernel, bf(*g0.shape), (g0, r2))
    g_in = exchange(final)
    return call(
        unpack_kernel,
        (out(rows, 2 * n * HEAD_SIZE),) * 2 + (out(rows, n * HEAD_SIZE),) * 2,
        (od_in, g_in),
        scratch=[dma((4 * n,))],
    )


def solution(mesh):
    seq, head = mesh.devices.shape
    kv_heads = 8
    lo = kv_heads // head
    inner = Mesh(mesh.devices.reshape(seq // lo, lo, head), ("hi", "lo", "head"))
    tokens = P(("hi", "lo", "head"), None)
    return jax.shard_map(
        body,
        mesh=inner,
        in_specs=(tokens,) * 4 + (P(("hi", "lo")),),
        out_specs=(tokens,) * 4,
        check_vma=False,
    )
```

```python
import functools

import jax
import jax.numpy as jnp
from jax import lax
from jax.experimental import pallas as pl
from jax.experimental.pallas import tpu as pltpu
from jax.sharding import Mesh, PartitionSpec as P

HEAD_SIZE = 128
BLOCK = 128
WBLOCKS = 8
LOG2E = 1.4426950408889634

query_scale = 168.0 ** (-0.5)
neg_fill = -1e30
EXTRA = 8

VM = pl.BlockSpec(memory_space=pltpu.VMEM)
HB = pl.BlockSpec(memory_space=pl.ANY)


def copy_all(pairs, sems):
    copies = [
        pltpu.make_async_copy(src, dst, sems.at[i]) for i, (src, dst) in enumerate(pairs)
    ]
    for copy in copies:
        copy.start()
    return copies


def pack_kernel(lo_ref, q_ref, k_ref, v_ref, g_ref, kv_ref, qg_ref, qg_s, lo_s, lo_sem, sems, out_sems):
    n, rows, _ = kv_ref.shape
    wide = q_ref.shape[1] // n
    fetch = pltpu.make_async_copy(lo_ref, lo_s, lo_sem)
    fetch.start()
    kv_pairs, qg_pairs = [], []
    for i in range(n):
        cols = slice(i * HEAD_SIZE, (i + 1) * HEAD_SIZE)
        kv_pairs.append((k_ref.at[:, cols], kv_ref.at[i, :, :HEAD_SIZE]))
        kv_pairs.append((v_ref.at[:, cols], kv_ref.at[i, :, HEAD_SIZE:]))
        cols = slice(i * wide, (i + 1) * wide)
        qg_pairs.append((q_ref.at[:, cols], qg_s.at[i, :rows, :wide]))
        qg_pairs.append((g_ref.at[:, cols], qg_s.at[i, :rows, wide:]))
    copies = copy_all(qg_pairs + kv_pairs, sems)
    fetch.wait()
    shards = lo_ref.shape[0]
    base = (lax.axis_index("hi") * lax.axis_size("lo") + lax.axis_index("lo")) * shards
    lane = lax.broadcasted_iota(jnp.int32, (EXTRA, 2 * wide), 1)
    told = jnp.zeros((EXTRA, 2 * wide), jnp.float32)
    for j in range(shards):
        back = (base + j - lo_s[j]).astype(jnp.float32)
        told = jnp.where(lane // BLOCK == j, back, told)
    outward = []
    for i in range(n):
        qg_s[i, rows:, :] = told.astype(jnp.bfloat16)
        copies[2 * i].wait()
        copies[2 * i + 1].wait()
        outward.append(pltpu.make_async_copy(qg_s.at[i], qg_ref.at[i], out_sems.at[i]))
        outward[i].start()
    for copy in copies[2 * n :] + outward:
        copy.wait()


def stacked(qg_ref, i, rows, first):
    per = BLOCK // rows
    return jnp.concatenate(
        [
            qg_ref[i * per : (i + 1) * per, :rows, j * HEAD_SIZE : (j + 1) * HEAD_SIZE].reshape(
                BLOCK, HEAD_SIZE
            )
            for j in (first, first + 1)
        ],
        axis=0,
    )


def nt(a, b):
    return lax.dot_general(a, b, (((1,), (1,)), ((), ())), preferred_element_type=jnp.float32)


def tn(a, b):
    return lax.dot_general(a, b, (((0,), (0,)), ((), ())), preferred_element_type=jnp.float32)


def nn(a, b):
    return jnp.dot(a, b, preferred_element_type=jnp.float32)


def spread(a, b):
    lane = lax.broadcasted_iota(jnp.int32, (a.shape[0], HEAD_SIZE), 1)
    return jnp.where(lane < HEAD_SIZE // 2, a, b)


def softmax_parts(s, cols, back, scale):
    col = lax.broadcasted_iota(jnp.int32, (2 * BLOCK, BLOCK), 1)
    row = lax.broadcasted_iota(jnp.int32, (2 * BLOCK, BLOCK), 0) % BLOCK
    parts = []
    for at, j in enumerate(cols):
        part = s[:, at * BLOCK : (at + 1) * BLOCK]
        if j == WBLOCKS:
            part = jnp.where(col <= row, part, neg_fill)
        else:
            part = part + jnp.where(back < WBLOCKS - j, neg_fill, 0.0)
        if j == 0:
            part = jnp.where(col > row, part, neg_fill)
        parts.append(part)
    top = jnp.max(functools.reduce(jnp.maximum, parts), axis=1, keepdims=True)
    parts = [jnp.exp2((part - top) * scale) for part in parts]
    total = jnp.sum(functools.reduce(jnp.add, parts), axis=1, keepdims=True)
    return jnp.concatenate(parts, axis=1), top, total


def blocks_back(qg_ref, i, rows, head_count):
    blocks = qg_ref.shape[0] * rows // BLOCK
    seq_blocks = head_count * rows // BLOCK
    owner = (i // seq_blocks) * head_count
    lane = (i % seq_blocks) * BLOCK
    back = qg_ref[owner, rows : rows + 1, lane : lane + 1].astype(jnp.float32)
    return jnp.minimum(back, (lax.axis_index("hi") * blocks + i).astype(jnp.float32))


def near_kernel(head_count, qg_ref, kv0_ref, kv1_ref, k_s, v_s, o_ref, p_ref, stat_ref):
    n, rows, _ = kv0_ref.shape
    tok = n * rows
    blocks = tok // BLOCK
    for part, ref in enumerate((kv1_ref, kv0_ref)):
        k_s[part * tok : (part + 1) * tok] = ref[:, :, :HEAD_SIZE].reshape(tok, HEAD_SIZE)
        v_s[part * tok : (part + 1) * tok] = ref[:, :, HEAD_SIZE:].reshape(tok, HEAD_SIZE)

    def step(i, start):
        keys = slice(start, tok + (i + 1) * BLOCK)
        count = keys.stop // BLOCK - start // BLOCK
        back = blocks_back(qg_ref, i, rows, head_count)
        s = nt(stacked(qg_ref, i, rows, 0), k_s[keys])
        e, top, total = softmax_parts(
            s, range(WBLOCKS + 1 - count, WBLOCKS + 1), back, query_scale * LOG2E
        )
        eb = e.astype(jnp.bfloat16)
        o_ref[i] = nn(eb, v_s[keys])
        p_ref[i, :, keys] = eb
        stat_ref[i] = spread(top, total)

    hi = lax.axis_index("hi")

    @pl.when(hi == 0)
    def _():
        for i in range(blocks):
            step(i, tok)

    @pl.when(hi > 0)
    def _():
        for i in range(blocks):
            step(i, 0)


def backward_step(i, start, refs, od_ref, dk_s, dv_s):
    qg_ref, k_s, v_s, kf_ref, o_ref, gs_ref, p_ref, dsf_ref, dots_ref = refs
    n, rows, _ = od_ref.shape
    tok = n * rows
    per = BLOCK // rows
    near = slice(start, tok + (i + 1) * BLOCK)
    q = stacked(qg_ref, i, rows, 0)
    g = gs_ref[i]
    pb = p_ref[i, :, near]
    dots = dots_ref[i, :, :1]
    ds = (pb.astype(jnp.float32) * (nt(g, v_s[near]) - dots)).astype(jnp.bfloat16)
    dq = nn(ds, k_s[near])
    if kf_ref is not None:
        dq = dq + nn(dsf_ref[i, :, : tok - i * BLOCK], kf_ref[i * BLOCK :])
    dq = (query_scale * dq).astype(jnp.bfloat16)
    o = o_ref[i]
    dk_s[near] += tn(ds, q)
    dv_s[near] += tn(pb, g)
    chunk = slice(i * per, (i + 1) * per)
    for u in range(2):
        part = slice(u * BLOCK, (u + 1) * BLOCK)
        od_ref[chunk, :, u * HEAD_SIZE : (u + 1) * HEAD_SIZE] = o[part].reshape(
            per, rows, HEAD_SIZE
        )
        od_ref[chunk, :, (2 + u) * HEAD_SIZE : (3 + u) * HEAD_SIZE] = dq[part].reshape(
            per, rows, HEAD_SIZE
        )


def hand_over(ref, dk, dv):
    n, rows, _ = ref.shape
    ref[:, :, :HEAD_SIZE] = (query_scale * dk).astype(ref.dtype).reshape(n, rows, HEAD_SIZE)
    ref[:, :, HEAD_SIZE:] = dv.astype(ref.dtype).reshape(n, rows, HEAD_SIZE)


def far_kernel(head_count, qg_ref, kv2_ref, near_ref, stat_ref, kn_ref, vn_ref, p_ref,
               k_s, o_ref, gs_ref, dsf_ref, dots_ref, g2_ref, od_ref, g1_ref, g0_ref,
               v_s, dk_s, dv_s):
    n, rows, _ = kv2_ref.shape
    tok = n * rows
    blocks = tok // BLOCK
    scale = query_scale * LOG2E

    def step(i, far_seen):
        q = stacked(qg_ref, i, rows, 0)
        g = stacked(qg_ref, i, rows, 2).astype(jnp.float32)
        top = stat_ref[i, :, :1]
        total = stat_ref[i, :, HEAD_SIZE // 2 : HEAD_SIZE // 2 + 1]
        if far_seen:
            far = slice(i * BLOCK, tok)
            width = tok - i * BLOCK
            back = blocks_back(qg_ref, i, rows, head_count)
            s = nt(q, k_s[far])
            e, far_top, far_total = softmax_parts(s, range(width // BLOCK), back, scale)
            eb = e.astype(jnp.bfloat16)
            most = jnp.maximum(top, far_top)
            near = jnp.exp2((top - most) * scale)
            away = jnp.exp2((far_top - most) * scale)
            share = 1.0 / (near * total + away * far_total)
            near = near * share
            away = away * share
            o = near_ref[i] * near + nn(eb, v_s[far]) * away
        else:
            near = 1.0 / total
            o = near_ref[i] * near
        o = o.astype(jnp.bfloat16)
        dots = jnp.sum(g * o.astype(jnp.float32), axis=1, keepdims=True)
        o_ref[i] = o
        gs_ref[i] = (g * near).astype(jnp.bfloat16)
        dots_ref[i] = jnp.broadcast_to(dots * near, (2 * BLOCK, HEAD_SIZE))
        if far_seen:
            g = (g * away).astype(jnp.bfloat16)
            ds = (e * (nt(g, v_s[far]) - dots * away)).astype(jnp.bfloat16)
            dsf_ref[i, :, :width] = ds
            dk_s[far] += tn(ds, q)
            dv_s[far] += tn(eb, g)

    hi = lax.axis_index("hi")

    @pl.when(hi == 0)
    def _():
        own = slice(tok, 2 * tok)
        dk_s[own] = jnp.zeros((tok, HEAD_SIZE), jnp.float32)
        dv_s[own] = jnp.zeros((tok, HEAD_SIZE), jnp.float32)
        refs = (qg_ref, kn_ref, vn_ref, None, o_ref, gs_ref, p_ref, None, dots_ref)
        for i in range(blocks):
            step(i, False)
            backward_step(i, tok, refs, od_ref, dk_s, dv_s)
        hand_over(g0_ref, dk_s[own], dv_s[own])
        g1_ref[...] = jnp.zeros_like(g1_ref)
        g2_ref[...] = jnp.zeros_like(g2_ref)

    @pl.when(hi > 0)
    def _():
        k_s[...] = kv2_ref[:, :, :HEAD_SIZE].reshape(tok, HEAD_SIZE)
        v_s[...] = kv2_ref[:, :, HEAD_SIZE:].reshape(tok, HEAD_SIZE)
        whole = slice(0, tok)
        dk_s[whole] = jnp.zeros((tok, HEAD_SIZE), jnp.float32)
        dv_s[whole] = jnp.zeros((tok, HEAD_SIZE), jnp.float32)
        for i in range(blocks):
            step(i, True)
        hand_over(g2_ref, dk_s[whole], dv_s[whole])


def backward_kernel(qg_ref, k_s, v_s, kf_ref, o_ref, gs_ref, p_ref, dsf_ref, dots_ref,
                    od_in, g1_in, g0_in, od_ref, g1_ref, g0_ref, dk_s, dv_s):
    n, rows, _ = od_ref.shape
    tok = n * rows
    refs = (qg_ref, k_s, v_s, kf_ref, o_ref, gs_ref, p_ref, dsf_ref, dots_ref)

    hi = lax.axis_index("hi")

    @pl.when(hi == 0)
    def _():
        od_ref[...] = od_in[...]
        g1_ref[...] = g1_in[...]
        g0_ref[...] = g0_in[...]

    @pl.when(hi > 0)
    def _():
        dk_s[...] = jnp.zeros_like(dk_s)
        dv_s[...] = jnp.zeros_like(dv_s)
        for i in range(tok // BLOCK):
            backward_step(i, 0, refs, od_ref, dk_s, dv_s)
        for part, ref in enumerate((g1_ref, g0_ref)):
            own = slice(part * tok, (part + 1) * tok)
            hand_over(ref, dk_s[own], dv_s[own])


def add_kernel(a_ref, b_ref, o_ref):
    o_ref[...] = (a_ref[...] + b_ref[...].astype(jnp.float32)).astype(jnp.bfloat16)


def unpack_kernel(a_ref, b_ref, o_ref, dq_ref, dk_ref, dv_ref, sems):
    pairs = []
    for ref, left, right in ((a_ref, o_ref, dq_ref), (b_ref, dk_ref, dv_ref)):
        wide = ref.shape[2] // 2
        for i in range(ref.shape[0]):
            cols = slice(i * wide, (i + 1) * wide)
            pairs.append((ref.at[i, :, :wide], left.at[:, cols]))
            pairs.append((ref.at[i, :, wide:], right.at[:, cols]))
    for copy in copy_all(pairs, sems):
        copy.wait()


def call(kernel, outs, args, scratch=(), outer=0, room=2):
    held = [
        pltpu.with_memory_space_constraint(x, pltpu.HBM if i < outer else pltpu.VMEM)
        for i, x in enumerate(args)
    ]
    return pl.pallas_call(
        kernel,
        out_shape=outs,
        in_specs=[HB] * outer + [VM] * (len(args) - outer),
        out_specs=jax.tree.map(
            lambda o: HB if isinstance(o, jax.ShapeDtypeStruct) else VM,
            outs,
            is_leaf=lambda o: not isinstance(o, tuple),
        ),
        scratch_shapes=list(scratch),
        compiler_params=pltpu.CompilerParams(vmem_limit_bytes=room << 20),
    )(*held)


def ring(x, by):
    n = lax.axis_size("hi")
    return lax.ppermute(x, "hi", [(i, (i + by) % n) for i in range(n)])


def line(x, by, least=0):
    n = lax.axis_size("hi")
    pairs = [(i, i + 1) for i in range(least, n - 1)]
    return lax.ppermute(x, "hi", pairs if by == 1 else [(j, i) for i, j in pairs])


def exchange(x):
    return lax.all_to_all(x, ("lo", "head"), split_axis=0, concat_axis=0, tiled=True)


def bf(*shape):
    return pltpu.VMEM(shape, jnp.bfloat16)


def f32(*shape):
    return pltpu.VMEM(shape, jnp.float32)


def out(*shape):
    return jax.ShapeDtypeStruct(shape, jnp.bfloat16)


def body(queries, keys, values, output_gradient, block_lo):
    rows = queries.shape[0]
    n = lax.axis_size("lo") * lax.axis_size("head")
    tok = n * rows
    blocks = tok // BLOCK
    heads = lax.axis_size("head")
    dma = pltpu.SemaphoreType.DMA

    kv_out, qg_out = call(
        pack_kernel,
        (bf(n, rows, 2 * HEAD_SIZE), out(n, rows + EXTRA, 4 * HEAD_SIZE)),
        (block_lo, queries, keys, values, output_gradient),
        scratch=[
            bf(n, rows + EXTRA, 4 * HEAD_SIZE),
            pltpu.SMEM(block_lo.shape, jnp.int32),
            dma,
            dma((4 * n,)),
            dma((n,)),
        ],
        outer=5,
    )
    kv0 = exchange(kv_out)
    kv1 = ring(kv0, 1)
    kv0, qg_out = lax.optimization_barrier((kv0, qg_out))
    qg = exchange(qg_out)
    kv2 = line(kv1, 1, 1)
    k_all, v_all, near, p, stat = call(
        functools.partial(near_kernel, heads),
        (
            bf(2 * tok, HEAD_SIZE),
            bf(2 * tok, HEAD_SIZE),
            f32(blocks, 2 * BLOCK, HEAD_SIZE),
            bf(blocks, 2 * BLOCK, 2 * tok),
            f32(blocks, 2 * BLOCK, HEAD_SIZE),
        ),
        (qg, kv0, kv1),
        room=20,
    )
    k_far, o, gs, dsf, dots, g2, od, g1, g0 = call(
        functools.partial(far_kernel, heads),
        (
            bf(tok, HEAD_SIZE),
            bf(blocks, 2 * BLOCK, HEAD_SIZE),
            bf(blocks, 2 * BLOCK, HEAD_SIZE),
            bf(blocks, 2 * BLOCK, tok),
            f32(blocks, 2 * BLOCK, HEAD_SIZE),
            bf(n, rows, 2 * HEAD_SIZE),
            bf(n, rows, 4 * HEAD_SIZE),
            f32(n, rows, 2 * HEAD_SIZE),
            f32(n, rows, 2 * HEAD_SIZE),
        ),
        (qg, kv2, near, stat, k_all, v_all, p),
        scratch=[bf(tok, HEAD_SIZE), f32(2 * tok, HEAD_SIZE), f32(2 * tok, HEAD_SIZE)],
        room=20,
    )
    r1 = ring(g2, -1)
    od, g1, g0 = call(
        backward_kernel,
        (
            bf(n, rows, 4 * HEAD_SIZE),
            f32(n, rows, 2 * HEAD_SIZE),
            f32(n, rows, 2 * HEAD_SIZE),
        ),
        (qg, k_all, v_all, k_far, o, gs, p, dsf, dots, od, g1, g0),
        scratch=[f32(2 * tok, HEAD_SIZE), f32(2 * tok, HEAD_SIZE)],
        room=24,
    )
    od_in = exchange(od)
    t = call(add_kernel, bf(*g1.shape), (g1, r1))
    r2 = ring(t, -1)
    final = call(add_kernel, bf(*g0.shape), (g0, r2))
    g_in = exchange(final)
    return call(
        unpack_kernel,
        (out(rows, 2 * n * HEAD_SIZE),) * 2 + (out(rows, n * HEAD_SIZE),) * 2,
        (od_in, g_in),
        scratch=[dma((4 * n,))],
    )


def solution(mesh):
    seq, head = mesh.devices.shape
    kv_heads = 8
    lo = kv_heads // head
    inner = Mesh(mesh.devices.reshape(seq // lo, lo, head), ("hi", "lo", "head"))
    tokens = P(("hi", "lo", "head"), None)
    return jax.shard_map(
        body,
        mesh=inner,
        in_specs=(tokens,) * 4 + (P(("hi", "lo")),),
        out_specs=(tokens,) * 4,
        check_vma=False,
    )
```
